32 devices in a mesh: grp: 2 (over y), seq: 8 (over z, x), mdl: 2 (over core).
Axes of the slice: x: 2, y: 2, z: 4, core: 2. Of those that a mesh axis runs over, the one named last changes fastest.
Arguments:
- signal: bfloat16 [2048, 2048], P(('grp', 'seq'), 'mdl'), parts along dimension 0, may hold values from -6 to 6
- gate_first: bfloat16 [2048, 2048], P(('grp', 'seq'), 'mdl'), parts along dimension 0, may hold values from -6 to 6
- gate_second: bfloat16 [2048, 2048], P(('grp', 'seq'), 'mdl'), parts along dimension 0, may hold values from -6 to 6
- spectrum_first: bfloat16 [2, 16, 128, 2048], P(None, 'seq', None, 'mdl'), may hold values from -8 to 8
- spectrum_second: bfloat16 [2, 16, 128, 2048], P(None, 'seq', None, 'mdl'), may hold values from -8 to 8
- skip_first: float32 [2048], P('mdl'), may hold values from 0.5 to 1.5
- skip_second: float32 [2048], P('mdl'), may hold values from 0.5 to 1.5
- out_weight: bfloat16 [2048, 2048], P('seq', 'mdl'), may hold values from -0.125 to 0.125
Outputs:
- block_out: bfloat16 [2048, 2048], P(('grp', 'seq'), 'mdl'), parts along dimension 0
The draws below stay inside these ranges and needn't reach their ends.
There are 2 independent parts, one for each index of `grp`. The reference program is written for one: setup_inputs(seed, part) draws one part's arguments, and reference() takes and returns one part's arrays. A program takes and returns all parts, laid end to end along the dimension named above; an argument that names none is the same for every part. Nothing has to cross between parts.
All inputs are finite; a program needn't handle non-finite values.
Results may differ from the reference program's by a relative error of at most 0.0057.
Values may be sent and summed in bfloat16 or wider, within the bound.
A program may use at most 64 MiB of HBM per device.

```python
import jax
import jax.numpy as jnp

D = 2048
S_DEV = 128
LENGTH = 1024
COARSE = 16


def level_of(rng, shape, cuts, smallest, high):
    loudness, own = 1.0, jax.random.fold_in(rng, 6)
    for axis_at, blocks in cuts:
        heights = jnp.exp(jax.random.uniform(jax.random.fold_in(own, axis_at), (blocks,), jnp.float32, smallest / len(cuts), high / len(cuts)))
        loudness = loudness * jnp.repeat(heights, shape[axis_at] // blocks).reshape([-1 if axis == axis_at else 1 for axis in range(len(shape))])
    return loudness


def normal_values(own_key, shape, scale, limit, split=(), dtype=jnp.bfloat16):
    array = jax.random.normal(own_key, shape, jnp.float32) * scale
    if len(split) > 0:
        array = level_of(own_key, shape, split, -0.22, 0.18) * array
    return jnp.clip(array, min=-limit, max=limit).astype(dtype)


def setup_inputs(seed: int = 0, part: int = 0) -> dict:
    streams_of = jax.random.split(jax.random.key(seed), 9)
    part_splits = jax.random.split(jax.random.fold_in(streams_of[8], part), 9)
    return {
        "signal": normal_values(part_splits[0], (LENGTH, D), 1.0, 6.0, ((0, 8), (1, 2))),
        "gate_first": normal_values(part_splits[1], (LENGTH, D), 1.0, 6.0, ((0, 8), (1, 2))),
        "gate_second": normal_values(part_splits[2], (LENGTH, D), 1.0, 6.0, ((0, 8), (1, 2))),
        "spectrum_first": normal_values(streams_of[3], (2, COARSE, S_DEV, D), 1.4, 8.0, ((1, 8), (3, 2))),
        "spectrum_second": normal_values(streams_of[4], (2, COARSE, S_DEV, D), 1.4, 8.0, ((1, 8), (3, 2))),
        "skip_first": jnp.clip(0.5 + 1.0 * jax.random.uniform(streams_of[5], (D,), jnp.float32) ** level_of(streams_of[5], (D,), ((0, 2),), -0.2, 0.2), 0.5, 1.5),
        "skip_second": jnp.clip(0.5 + 1.0 * jax.random.uniform(streams_of[6], (D,), jnp.float32) ** level_of(streams_of[6], (D,), ((0, 2),), -0.2, 0.2), 0.5, 1.5),
        "out_weight": normal_values(streams_of[7], (D, D), D ** -0.5, 0.125, ((0, 8), (1, 2))),
    }


def long_filter(field, spectrum):
    total = field.shape[0]
    coarse = spectrum.shape[1]
    fine = spectrum.shape[2]
    width = field.shape[1]
    spec_re = spectrum[0].astype(jnp.float32).transpose(1, 0, 2).reshape(coarse * fine, width)
    spec_im = spectrum[1].astype(jnp.float32).transpose(1, 0, 2).reshape(coarse * fine, width)
    block = 256 if width % 256 == 0 else width
    pieces = []
    for start in range(0, width, block):
        part = field[:, start:start + block]
        padded = jnp.concatenate([part, jnp.zeros_like(part)], axis=0)
        spectra = jnp.fft.fft(padded, axis=0)
        spectra = spectra * (spec_re[:, start:start + block] + 1j * spec_im[:, start:start + block])
        back = jnp.real(jnp.fft.ifft(spectra, axis=0))[:total]
        pieces.append(back)
    return jnp.concatenate(pieces, axis=1)


def reference(signal, gate_first, gate_second, spectrum_first, spectrum_second, skip_first, skip_second, out_weight):
    values = signal.astype(jnp.float32)
    first_conv = long_filter(values, spectrum_first) + skip_first[None, :] * values
    first_out = (gate_first.astype(jnp.float32) * first_conv).astype(jnp.bfloat16)
    first_vals = first_out.astype(jnp.float32)
    second_conv = long_filter(first_vals, spectrum_second) + skip_second[None, :] * first_vals
    mixed = (gate_second.astype(jnp.float32) * second_conv).astype(jnp.bfloat16)
    return jnp.dot(mixed, out_weight, preferred_element_type=jnp.float32).astype(jnp.bfloat16)
```

```python
import functools
import math

import jax
import jax.numpy as jnp
import numpy as np
from jax import lax
from jax.experimental import pallas as pl
from jax.experimental.pallas import tpu as pltpu
from jax.sharding import PartitionSpec as P

MESH = pl.DeviceIdType.MESH
LANES = 128


def angle_grid(first, second, modulus):
    product = first[:, None] * second[None, :] % modulus
    angles = product.astype(jnp.float32) * (2.0 * math.pi / modulus)
    return (jnp.cos(angles), jnp.sin(angles))


def mixing(form, left, right):
    return jnp.einsum(form, left, right, precision=lax.Precision.HIGHEST)


def complex_mix(form, real_table, imag_table, values_re, values_im):
    first_term = mixing(form, real_table, values_re + values_im)
    second_term = mixing(form, real_table + imag_table, values_im)
    third_term = mixing(form, imag_table - real_table, values_re)
    return (first_term - second_term, first_term + third_term)


def channel_filter(field, spectrum):
    coarse = spectrum.shape[1]
    span = spectrum.shape[2]
    count = coarse // 2
    cols = field.shape[1]
    length = coarse * span
    pencil = field.reshape(count, span, cols)
    coarse_ids = jnp.arange(coarse, dtype=jnp.int32)
    cos_a, sin_a = angle_grid(coarse_ids, jnp.arange(count, dtype=jnp.int32), coarse)
    part_re = mixing("ka,amc->kmc", cos_a, pencil)
    part_im = -mixing("ka,amc->kmc", sin_a, pencil)
    fine_ids = jnp.arange(span, dtype=jnp.int32)
    cos_t, sin_t = angle_grid(coarse_ids, fine_ids, length)
    cos_t = cos_t[:, :, None]
    sin_t = sin_t[:, :, None]
    turned_re = part_re * cos_t + part_im * sin_t
    turned_im = part_im * cos_t - part_re * sin_t
    cos_s, sin_s = angle_grid(fine_ids, fine_ids, span)
    full_re, full_im = complex_mix("qm,kmc->kqc", cos_s, -sin_s, turned_re, turned_im)
    filt_re = spectrum[0].astype(jnp.float32)
    filt_im = spectrum[1].astype(jnp.float32)
    prod_re = filt_re * full_re - filt_im * full_im
    prod_im = filt_re * full_im + filt_im * full_re
    inner_re, inner_im = complex_mix("mq,kqc->kmc", cos_s, sin_s, prod_re, prod_im)
    back_re = inner_re * cos_t - inner_im * sin_t
    back_im = inner_im * cos_t + inner_re * sin_t
    result = mixing("ka,kmc->amc", cos_a, back_re) - mixing("ka,kmc->amc", sin_a, back_im)
    return (result / length).reshape(count * span, cols)


def plain_shards(
    signal,
    gate_first,
    gate_second,
    spectrum_first,
    spectrum_second,
    skip_first,
    skip_second,
    out_weight,
):
    seq_index = lax.axis_index("seq")
    width = signal.shape[1]
    parts_seq = lax.axis_size("seq")
    cols = width // parts_seq
    col_sig, col_first, col_second = (
        lax.all_to_all(signal, "seq", split_axis=1, concat_axis=0, tiled=True),
        lax.all_to_all(gate_first, "seq", split_axis=1, concat_axis=0, tiled=True),
        lax.all_to_all(gate_second, "seq", split_axis=1, concat_axis=0, tiled=True),
    )
    spec_one, spec_two = (
        lax.all_to_all(spectrum_first, "seq", split_axis=3, concat_axis=1, tiled=True),
        lax.all_to_all(spectrum_second, "seq", split_axis=3, concat_axis=1, tiled=True),
    )
    skip_one = lax.dynamic_slice_in_dim(skip_first, seq_index * cols, cols, 0)
    skip_two = lax.dynamic_slice_in_dim(skip_second, seq_index * cols, cols, 0)
    values = col_sig.astype(jnp.float32)
    first_conv = channel_filter(values, spec_one) + skip_one * values
    first_out = (col_first.astype(jnp.float32) * first_conv).astype(jnp.bfloat16)
    first_vals = first_out.astype(jnp.float32)
    second_conv = channel_filter(first_vals, spec_two) + skip_two * first_vals
    mixed_cols = (col_second.astype(jnp.float32) * second_conv).astype(jnp.bfloat16)
    mixed = lax.all_to_all(mixed_cols, "seq", split_axis=0, concat_axis=1, tiled=True)
    features = lax.all_gather(mixed, "mdl", axis=1, tiled=True)
    total = jnp.dot(
        features,
        lax.all_gather(out_weight, "seq", axis=0, tiled=True),
        preferred_element_type=jnp.float32,
    )
    return total.astype(jnp.bfloat16)


def turn_tables(span, coarse):
    ids = np.arange(span)
    fine = 2.0 * math.pi * (ids[:, None] * ids[None, :] % span) / span
    step = 2.0 * math.pi * np.broadcast_to(ids[:, None], (span, span)) / (span * coarse)
    return np.stack(
        [np.cos(fine), np.sin(fine), np.cos(step), np.sin(step), np.cos(step).T, np.sin(step).T]
    ).astype(np.float32)


def weighted(terms):
    total = None
    for weight, value in terms:
        if abs(weight) < 1e-12:
            continue
        if abs(weight - 1.0) < 1e-12:
            term = value
        elif abs(weight + 1.0) < 1e-12:
            total = -value if total is None else total - value
            continue
        else:
            term = value * weight
        total = term if total is None else total + term
    return total


def coarse_forward(field, parts, rows):
    count, span, cols = field.shape
    half = count // 2

    @pl.loop(0, span // rows)
    def _(i):
        at = pl.multiple_of(i * rows, rows)
        f = [field[a, pl.ds(at, rows), :].astype(jnp.float32) for a in range(count)]
        plus = {a: f[a] + f[count - a] for a in range(1, half)}
        minus = {a: f[a] - f[count - a] for a in range(1, half)}
        for j in range(count + 1):
            for_cos, for_sin = (plus, minus) if j % 2 == 0 else (minus, plus)
            angle = [math.pi * a * j / count for a in range(count)]
            real = weighted(
                [(1.0, f[0]), (math.cos(angle[half]), f[half])]
                + [(math.cos(angle[a]), for_cos[a]) for a in range(1, half)]
            )
            imag = weighted(
                [(-math.sin(angle[half]), f[half])]
                + [(-math.sin(angle[a]), for_sin[a]) for a in range(1, half)]
            )
            if imag is None:
                imag = jnp.zeros_like(real)
            for top, value in ((at, real), (pl.multiple_of(span + at, rows), imag)):
                high = value.astype(jnp.bfloat16)
                parts[j, pl.ds(top, rows), :cols] = high
                parts[j, pl.ds(top, rows), cols:] = (value - high.astype(jnp.float32)).astype(
                    jnp.bfloat16
                )


def split_dot(table, j, both, cols):
    main = jnp.dot(table[j, 0], both, preferred_element_type=jnp.float32)
    rest = jnp.dot(table[j, 1], both[:, :cols], preferred_element_type=jnp.float32)
    return main[:, :cols] + (main[:, cols:] + rest)


def fine_stage(parts, spectrum, there, back_table, back, own, arrive, pass_over, passed):
    half = back.shape[0] // 2
    span, cols = spectrum.shape[3], spectrum.shape[4]

    def one(k, b):
        j = 2 * b + k
        source = jnp.where(j <= half, j, 2 * half - j)
        full = split_dot(there, j, parts[source], cols)
        full_re, full_im = full[:span], full[span:]
        filt_re = spectrum[k, b, 0].astype(jnp.float32)
        filt_im = spectrum[k, b, 1].astype(jnp.float32)
        prod_re = filt_re * full_re - filt_im * full_im
        prod_im = filt_re * full_im + filt_im * full_re
        prod = jnp.concatenate([prod_re, prod_im], axis=0)
        high = prod.astype(jnp.bfloat16)
        low = (prod - high.astype(jnp.float32)).astype(jnp.bfloat16)
        both = jnp.concatenate([high, low], axis=1)
        back[j] = split_dot(back_table, j, both, cols)

    @pl.loop(0, half // 2)
    def _(v):
        blocks = arrive(v)
        for b in blocks:
            pass_over(b)
        for b in blocks:
            one(own, b)
        for b in blocks:
            passed(b)
        for b in blocks:
            one(1 - own, b)


def coarse_back(back, field, gate, skip, result, rows, first, last):
    count, span, cols = field.shape
    half = count // 2
    direct = jnp.broadcast_to(skip, (rows, cols))

    @pl.loop(first // rows, last // rows)
    def _(i):
        at = pl.multiple_of(i * rows, rows)
        low = pl.multiple_of(span + at, rows)

        def real(j):
            return back[j, pl.ds(at, rows), :]

        def imag(j):
            return back[j, pl.ds(low, rows), :]

        re = [real(0)] + [real(j) + real(2 * count - j) for j in range(1, count)] + [real(count)]
        im = [None] + [imag(j) - imag(2 * count - j) for j in range(1, count)] + [None]
        even_re = [re[j] + re[count - j] for j in range(half)]
        odd_re = [re[j] - re[count - j] for j in range(half)]
        even_im = [None] + [im[j] - im[count - j] for j in range(1, half)]
        odd_im = [None] + [im[j] + im[count - j] for j in range(1, half)]
        for a in range(count):
            use_re, use_im = (even_re, even_im) if a % 2 == 0 else (odd_re, odd_im)
            angle = [math.pi * a * j / count for j in range(half + 1)]
            total = weighted(
                [(math.cos(angle[j]), use_re[j]) for j in range(half)]
                + [(math.cos(angle[half]), re[half]), (-math.sin(angle[half]), im[half])]
                + [(-math.sin(angle[j]), use_im[j]) for j in range(1, half)]
            )
            values = field[a, pl.ds(at, rows), :].astype(jnp.float32)
            total = total + direct * values
            if gate is not None:
                total = gate[a, pl.ds(at, rows), :].astype(jnp.float32) * total
            result[a, pl.ds(at, rows), :] = total.astype(jnp.bfloat16)


def build_tables(tab, there, back_table, turn, count, span):
    turn[0] = tab[0]
    turn[1] = tab[1]
    turn[2] = tab[0]
    turn[3] = tab[1]
    scale = 1.0 / (2 * count * span)

    @pl.loop(0, 2 * count)
    def _(j):
        flip = jnp.where(j > count, -1.0, 1.0).astype(jnp.float32)
        cos_a, sin_a, cos_b, sin_b = turn[0], turn[1], turn[2], turn[3]
        cos_s, sin_s = cos_b * scale, sin_b * scale
        entries = (
            (there, cos_a, sin_a * flip, -sin_a, cos_a * flip),
            (back_table, cos_s, -sin_s, sin_s, cos_s),
        )
        places = ((0, 0), (0, 1), (1, 0), (1, 1))
        for table, *blocks in entries:
            for (row, col), value in zip(places, blocks):
                at = (slice(row * span, row * span + span), slice(col * span, col * span + span))
                high = value.astype(jnp.bfloat16)
                table[(j, 0) + at] = high
                table[(j, 1) + at] = (value - high.astype(jnp.float32)).astype(jnp.bfloat16)
        turn[0] = cos_a * tab[4] - sin_a * tab[5]
        turn[1] = sin_a * tab[4] + cos_a * tab[5]
        turn[2] = cos_b * tab[2] - sin_b * tab[3]
        turn[3] = sin_b * tab[2] + cos_b * tab[3]


def block_kernel(
    count,
    signal,
    gate_one,
    gate_two,
    spec_one,
    spec_two,
    skip_one,
    skip_two,
    weight,
    tab,
    out,
    in_signal,
    in_gate_one,
    in_gate_two,
    in_spec_one,
    in_spec_two,
    in_skip,
    there,
    back_table,
    turn,
    parts,
    back,
    second_field,
    mixed,
    arrived,
    features,
    totals,
    to_other,
    from_other,
    rows_all,
    send_sem,
    own_sem,
    recv_sem,
    spec_recv,
    relay_recv,
    weight_recv,
    mix_recv,
    pass_recv,
    other_recv,
):
    g, s, m = lax.axis_index("grp"), lax.axis_index("seq"), lax.axis_index("mdl")
    span, cols = in_signal.shape[1], in_signal.shape[2]
    total = 4 * count
    levels = count // 2
    z, x = s // 2, lax.rem(s, 2)
    me = (g * count + s) * 2 + m

    barrier = pltpu.get_barrier_semaphore()

    @pl.loop(1, total)
    def _(o):
        peer = lax.rem(me + o, total)
        pl.semaphore_signal(
            barrier,
            inc=1,
            device_id=(peer // (2 * count), lax.rem(peer // 2, count), lax.rem(peer, 2)),
            device_id_type=MESH,
        )

    pl.semaphore_wait(barrier, total - 1)

    def level(v):
        return 2 * lax.rem(z // 2 + v // 2, 2) + lax.rem(z + v, 2)

    def columns(block):
        return pl.ds(pl.multiple_of(block * cols, cols), cols)

    def remote(source, target, send, recv, where):
        return pltpu.make_async_remote_copy(
            src_ref=source,
            dst_ref=target,
            send_sem=send,
            recv_sem=recv,
            device_id=where,
            device_id_type=MESH,
        )

    def local(source, target, recv):
        return pltpu.make_async_copy(source, target, recv)

    def take(view, sem):
        pltpu.make_async_copy(view, view, sem).wait()

    own_here = (g == m) & (x == m)

    def send_rows(array, buffer, slot):
        for v in (2, 3, 1, 0):
            to_z = level(v)
            for away in (1, 0):
                plane = g if away == 0 else 1 - g
                source = array.at[:, columns(2 * to_z + plane)]
                where = (plane, 2 * to_z + m, g)
                if v or away:
                    remote(
                        source, buffer.at[s], send_sem.at[slot], recv_sem.at[slot], where
                    ).start()
                    continue

                @pl.when(own_here)
                def _():
                    local(source, buffer.at[s], recv_sem.at[slot]).start()

                @pl.when(jnp.logical_not(own_here))
                def _():
                    remote(
                        source, buffer.at[s], own_sem.at[slot], recv_sem.at[slot], where
                    ).start()

    def send_spectrum(array, buffer, slot, which):
        for v in (2, 3, 1, 0):
            to_z = level(v)
            for other in (1, 0):
                k = 1 - m if other else m
                source = array.at[:, k, :, columns(2 * to_z + g)]
                target = buffer.at[k, s]
                recv = spec_recv.at[which, s]
                where = (g, 2 * to_z + m, k)
                if v or other:
                    remote(source, target, send_sem.at[slot], recv, where).start()
                    continue

                @pl.when(x == m)
                def _():
                    local(source, target, recv).start()

                @pl.when(x != m)
                def _():
                    remote(source, target, own_sem.at[slot], recv, where).start()

    def send_gate_two():
        for v in range(levels):
            source = gate_two.at[:, columns(2 * v + 1 - g)]
            target = in_gate_two.at[:, columns(levels * m + v)]
            remote(source, target, send_sem.at[4], recv_sem.at[4], (1 - g, s, g)).start()

            source = gate_two.at[:, columns(2 * v + g)]

            @pl.when(g == m)
            def _():
                local(source, target, recv_sem.at[4]).start()

            @pl.when(g != m)
            def _():
                remote(source, target, own_sem.at[4], recv_sem.at[4], (g, s, g)).start()

    def send_skips():
        @pl.when(x == m)
        def _():
            for at, skip in enumerate((skip_one, skip_two)):
                local(skip, in_skip.at[at], recv_sem.at[5]).start()
                remote(
                    skip, in_skip.at[at], own_sem.at[5], recv_sem.at[5], (g, s, 1 - m)
                ).start()

    depth = weight.shape[0] // 2
    piece = depth // 2
    beside = s + 1 - 2 * x

    def chunk(block, p):
        return rows_all.at[pl.ds(pl.multiple_of(block * depth + p * piece, piece), piece), :]

    def on_line(v):
        return 2 * level(v) + x

    def post(block, p, source, where, slot):
        remote(
            source, chunk(block, p), send_sem.at[11], weight_recv.at[p, slot], (g, where, m)
        ).start()

    def landed(block, p, slot):
        take(chunk(block, p), weight_recv.at[p, slot])

    def weight_own(p):
        source = weight.at[pl.ds(pl.multiple_of(g * depth + p * piece, piece), piece), :]
        post(s, p, source, on_line(2), 2)
        post(s, p, source, on_line(1), 1)
        post(s, p, source, beside, 4)
        local(source, chunk(s, p), weight_recv.at[p, 0]).start()

    def weight_near(p):
        block = on_line(1)
        landed(block, p, 1)
        post(block, p, chunk(block, p), beside, 5)

    def weight_far(p):
        block = on_line(2)
        landed(block, p, 2)
        post(block, p, chunk(block, p), on_line(1), 3)
        post(block, p, chunk(block, p), beside, 6)

    def weight_last(p):
        block = on_line(3)
        landed(block, p, 3)
        post(block, p, chunk(block, p), beside, 7)

    def weight_end():
        for p in range(2):
            landed(s, p, 0)
            for v in range(levels):
                landed(2 * level(v) + 1 - x, p, 4 + v)

    def relay(buffer, which, b):
        return remote(
            buffer.at[m, b],
            buffer.at[m, b],
            send_sem.at[6 + which],
            relay_recv.at[which, b],
            (g, s, 1 - m),
        )

    def fine(buffer, which):
        def arrive(v):
            blocks = (2 * level(v) + x, 2 * level(v) + 1 - x)
            for b in blocks:
                take(buffer.at[m, b], spec_recv.at[which, b])
            return blocks

        def pass_over(b):
            relay(buffer, which, b).start()

        def passed(b):
            take(buffer.at[1 - m, b], relay_recv.at[which, b])

        fine_stage(parts, buffer, there, back_table, back, m, arrive, pass_over, passed)

    weight_own(0)
    weight_own(1)
    send_rows(signal, in_signal, 0)
    send_spectrum(spec_one, in_spec_one, 2, 0)
    build_tables(tab, there, back_table, turn, count, span)
    weight_near(0)
    weight_near(1)
    weight_far(0)
    weight_far(1)
    send_rows(gate_one, in_gate_one, 1)
    weight_last(0)
    weight_last(1)
    send_spectrum(spec_two, in_spec_two, 3, 1)
    send_gate_two()
    send_skips()
    take(in_signal, recv_sem.at[0])
    coarse_forward(in_signal, parts, 16)
    fine(in_spec_one, 0)
    take(in_gate_one, recv_sem.at[1])
    take(in_skip, recv_sem.at[5])
    mine = pl.ds(2 * z + g, 1)
    coarse_back(back, in_signal, in_gate_one, in_skip[0, mine, :], second_field, 16, 0, span)
    coarse_forward(second_field, parts, 16)
    fine(in_spec_two, 1)

    rows = span // mix_recv.shape[0]
    place = columns(levels * x + z)

    def strip(r):
        return pl.ds(r * rows, rows)

    for r in range(span // rows):
        skip = in_skip[1, mine, :]
        coarse_back(back, second_field, None, skip, mixed, 16, r * rows, r * rows + rows)
        for v in (2, 3, 1, 0):
            for side in (0, 1):
                to = 2 * level(v) + (1 - x if side == 0 else x)
                source = mixed.at[to, strip(r), :]
                target = arrived.at[strip(r), place]
                if v or side == 0:
                    remote(source, target, send_sem.at[8], mix_recv.at[r], (g, to, m)).start()
                else:
                    local(source, target, mix_recv.at[r]).start()

    take(in_gate_two, recv_sem.at[4])
    weight_end()

    def hand_over(r):
        view = features.at[m, strip(r), :]
        return remote(view, view, send_sem.at[9], pass_recv.at[r], (g, s, 1 - m))

    def exchange(r):
        source, target = to_other.at[strip(r), :], from_other.at[strip(r), :]
        return remote(source, target, send_sem.at[10], other_recv.at[r], (1 - g, s, m))

    width = count * cols
    tile = 2 * cols
    for r in range(span // rows):
        take(arrived.at[strip(r), :], mix_recv.at[r])
        gated = in_gate_two[strip(r), :].astype(jnp.float32) * arrived[strip(r), :].astype(
            jnp.float32
        )
        features[m, strip(r), :] = gated.astype(jnp.bfloat16)
        hand_over(r).start()
        take(features.at[1 - m, strip(r), :], pass_recv.at[r])

        @pl.loop(0, width // tile)
        def _(i):
            at = pl.ds(pl.multiple_of(i * tile, tile), tile)
            both = jnp.concatenate(
                [features[1 - g, strip(r), :], features[g, strip(r), :]], axis=0
            )
            sums = jnp.dot(both, rows_all[:, at], preferred_element_type=jnp.float32)
            to_other[strip(r), at] = sums[:rows].astype(jnp.bfloat16)
            totals[strip(r), at] = sums[rows:]

        exchange(r).start()

    for r in range(span // rows):
        take(from_other.at[strip(r), :], other_recv.at[r])
        more = from_other[strip(r), :].astype(jnp.float32)
        out[strip(r), :] = (totals[strip(r), :] + more).astype(out.dtype)

    most = pl.ds(0, count - 1)
    take(in_signal.at[most], send_sem.at[0])
    take(in_signal.at[most], send_sem.at[1])
    for which in range(2):
        take(in_spec_one.at[0, most], send_sem.at[2 + which])
        take(in_spec_one.at[0], send_sem.at[6 + which])
    half_gate = in_gate_two.at[:, pl.ds(0, width // 2)]
    take(half_gate, send_sem.at[4])
    take(in_signal.at[most], send_sem.at[8])
    take(arrived, send_sem.at[9])
    take(arrived, send_sem.at[10])
    take(rows_all.at[pl.ds(0, 7 * depth), :], send_sem.at[11])

    @pl.when(jnp.logical_not(own_here))
    def _():
        take(in_signal.at[0], own_sem.at[0])
        take(in_signal.at[0], own_sem.at[1])

    @pl.when(x != m)
    def _():
        take(in_spec_one.at[0, 0], own_sem.at[2])
        take(in_spec_one.at[0, 0], own_sem.at[3])

    @pl.when(x == m)
    def _():
        take(in_skip, own_sem.at[5])

    @pl.when(g != m)
    def _():
        take(half_gate, own_sem.at[4])


def direct_shards(
    signal,
    gate_first,
    gate_second,
    spectrum_first,
    spectrum_second,
    skip_first,
    skip_second,
    out_weight,
):
    count = lax.axis_size("seq")
    span, width = signal.shape
    cols = width // count
    coarse = 2 * count
    strips = 2
    anywhere = pl.BlockSpec(memory_space=pltpu.HBM)
    vmem = pl.BlockSpec(memory_space=pltpu.VMEM)
    bf16, f32 = jnp.bfloat16, jnp.float32
    return pl.pallas_call(
        functools.partial(block_kernel, count),
        out_shape=jax.ShapeDtypeStruct((span, width), bf16),
        in_specs=[anywhere] * 8 + [vmem],
        out_specs=vmem,
        scratch_shapes=[
            pltpu.VMEM((count, span, cols), bf16),
            pltpu.VMEM((count, span, cols), bf16),
            pltpu.VMEM((span, width), bf16),
            pltpu.VMEM((2, count, 2, span, cols), bf16),
            pltpu.VMEM((2, count, 2, span, cols), bf16),
            pltpu.VMEM((2, count, cols), f32),
            pltpu.VMEM((coarse, 2, 2 * span, 2 * span), bf16),
            pltpu.VMEM((coarse, 2, 2 * span, 2 * span), bf16),
            pltpu.VMEM((4, span, span), f32),
            pltpu.VMEM((count + 1, 2 * span, 2 * cols), bf16),
            pltpu.VMEM((coarse, 2 * span, cols), f32),
            pltpu.VMEM((count, span, cols), bf16),
            pltpu.VMEM((count, span, cols), bf16),
            pltpu.VMEM((span, width), bf16),
            pltpu.VMEM((2, span, width), bf16),
            pltpu.VMEM((span, width), f32),
            pltpu.VMEM((span, width), bf16),
            pltpu.VMEM((span, width), bf16),
            pltpu.VMEM((width, width), bf16),
            pltpu.SemaphoreType.DMA((12,)),
            pltpu.SemaphoreType.DMA((6,)),
            pltpu.SemaphoreType.DMA((6,)),
            pltpu.SemaphoreType.DMA((2, count)),
            pltpu.SemaphoreType.DMA((2, count)),
            pltpu.SemaphoreType.DMA((2, count)),
            pltpu.SemaphoreType.DMA((strips,)),
            pltpu.SemaphoreType.DMA((strips,)),
            pltpu.SemaphoreType.DMA((strips,)),
        ],
        compiler_params=pltpu.CompilerParams(
            collective_id=0, has_side_effects=True, vmem_limit_bytes=62 * 1024 * 1024
        ),
        cost_estimate=pl.CostEstimate(
            flops=16 * coarse * span * span * cols, bytes_accessed=1 << 26, transcendentals=0
        ),
    )(
        signal,
        gate_first,
        gate_second,
        spectrum_first,
        spectrum_second,
        skip_first.reshape(count, cols),
        skip_second.reshape(count, cols),
        out_weight,
        jnp.asarray(turn_tables(span, coarse)),
    )


def shards(*arrays):
    count = lax.axis_size("seq")
    span, width = arrays[0].shape
    pairs = lax.axis_size("grp") == 2 and lax.axis_size("mdl") == 2
    whole_tiles = width == count * LANES and span == LANES and count == 8
    if pairs and whole_tiles and arrays[3].shape[1] == 2:
        return direct_shards(*arrays)
    return plain_shards(*arrays)


def solution(mesh):
    placed = (
        P(("grp", "seq"), "mdl"),
        P(("grp", "seq"), "mdl"),
        P(("grp", "seq"), "mdl"),
        P(None, "seq", None, "mdl"),
        P(None, "seq", None, "mdl"),
        P("mdl"),
        P("mdl"),
        P("seq", "mdl"),
    )
    return jax.shard_map(
        shards, mesh=mesh, in_specs=placed, out_specs=P(("grp", "seq"), "mdl"), check_vma=False
    )
```

```python
import functools
import math

import jax
import jax.numpy as jnp
import numpy as np
from jax import lax
from jax.experimental import pallas as pl
from jax.experimental.pallas import tpu as pltpu
from jax.sharding import PartitionSpec as P

MESH = pl.DeviceIdType.MESH
LANES = 128


def angle_grid(first, second, modulus):
    product = first[:, None] * second[None, :] % modulus
    angles = product.astype(jnp.float32) * (2.0 * math.pi / modulus)
    return (jnp.cos(angles), jnp.sin(angles))


def mixing(form, left, right):
    return jnp.einsum(form, left, right, precision=lax.Precision.HIGHEST)


def complex_mix(form, real_table, imag_table, values_re, values_im):
    first_term = mixing(form, real_table, values_re + values_im)
    second_term = mixing(form, real_table + imag_table, values_im)
    third_term = mixing(form, imag_table - real_table, values_re)
    return (first_term - second_term, first_term + third_term)


def channel_filter(field, spectrum):
    coarse = spectrum.shape[1]
    span = spectrum.shape[2]
    count = coarse // 2
    cols = field.shape[1]
    length = coarse * span
    pencil = field.reshape(count, span, cols)
    coarse_ids = jnp.arange(coarse, dtype=jnp.int32)
    cos_a, sin_a = angle_grid(coarse_ids, jnp.arange(count, dtype=jnp.int32), coarse)
    part_re = mixing("ka,amc->kmc", cos_a, pencil)
    part_im = -mixing("ka,amc->kmc", sin_a, pencil)
    fine_ids = jnp.arange(span, dtype=jnp.int32)
    cos_t, sin_t = angle_grid(coarse_ids, fine_ids, length)
    cos_t = cos_t[:, :, None]
    sin_t = sin_t[:, :, None]
    turned_re = part_re * cos_t + part_im * sin_t
    turned_im = part_im * cos_t - part_re * sin_t
    cos_s, sin_s = angle_grid(fine_ids, fine_ids, span)
    full_re, full_im = complex_mix("qm,kmc->kqc", cos_s, -sin_s, turned_re, turned_im)
    filt_re = spectrum[0].astype(jnp.float32)
    filt_im = spectrum[1].astype(jnp.float32)
    prod_re = filt_re * full_re - filt_im * full_im
    prod_im = filt_re * full_im + filt_im * full_re
    inner_re, inner_im = complex_mix("mq,kqc->kmc", cos_s, sin_s, prod_re, prod_im)
    back_re = inner_re * cos_t - inner_im * sin_t
    back_im = inner_im * cos_t + inner_re * sin_t
    result = mixing("ka,kmc->amc", cos_a, back_re) - mixing("ka,kmc->amc", sin_a, back_im)
    return (result / length).reshape(count * span, cols)


def plain_shards(
    signal,
    gate_first,
    gate_second,
    spectrum_first,
    spectrum_second,
    skip_first,
    skip_second,
    out_weight,
):
    seq_index = lax.axis_index("seq")
    width = signal.shape[1]
    parts_seq = lax.axis_size("seq")
    cols = width // parts_seq
    col_sig, col_first, col_second = (
        lax.all_to_all(signal, "seq", split_axis=1, concat_axis=0, tiled=True),
        lax.all_to_all(gate_first, "seq", split_axis=1, concat_axis=0, tiled=True),
        lax.all_to_all(gate_second, "seq", split_axis=1, concat_axis=0, tiled=True),
    )
    spec_one, spec_two = (
        lax.all_to_all(spectrum_first, "seq", split_axis=3, concat_axis=1, tiled=True),
        lax.all_to_all(spectrum_second, "seq", split_axis=3, concat_axis=1, tiled=True),
    )
    skip_one = lax.dynamic_slice_in_dim(skip_first, seq_index * cols, cols, 0)
    skip_two = lax.dynamic_slice_in_dim(skip_second, seq_index * cols, cols, 0)
    values = col_sig.astype(jnp.float32)
    first_conv = channel_filter(values, spec_one) + skip_one * values
    first_out = (col_first.astype(jnp.float32) * first_conv).astype(jnp.bfloat16)
    first_vals = first_out.astype(jnp.float32)
    second_conv = channel_filter(first_vals, spec_two) + skip_two * first_vals
    mixed_cols = (col_second.astype(jnp.float32) * second_conv).astype(jnp.bfloat16)
    mixed = lax.all_to_all(mixed_cols, "seq", split_axis=0, concat_axis=1, tiled=True)
    features = lax.all_gather(mixed, "mdl", axis=1, tiled=True)
    total = jnp.dot(
        features,
        lax.all_gather(out_weight, "seq", axis=0, tiled=True),
        preferred_element_type=jnp.float32,
    )
    return total.astype(jnp.bfloat16)


def turn_tables(span, coarse):
    ids = np.arange(span)
    fine = 2.0 * math.pi * (ids[:, None] * ids[None, :] % span) / span
    step = 2.0 * math.pi * np.broadcast_to(ids[:, None], (span, span)) / (span * coarse)
    return np.stack(
        [np.cos(fine), np.sin(fine), np.cos(step), np.sin(step), np.cos(step).T, np.sin(step).T]
    ).astype(np.float32)


def weighted(terms):
    total = None
    for weight, value in terms:
        if abs(weight) < 1e-12:
            continue
        if abs(weight - 1.0) < 1e-12:
            term = value
        elif abs(weight + 1.0) < 1e-12:
            total = -value if total is None else total - value
            continue
        else:
            term = value * weight
        total = term if total is None else total + term
    return total


def coarse_forward(field, parts, rows):
    count, span, cols = field.shape
    half = count // 2

    @pl.loop(0, span // rows)
    def _(i):
        at = pl.multiple_of(i * rows, rows)
        f = [field[a, pl.ds(at, rows), :].astype(jnp.float32) for a in range(count)]
        plus = {a: f[a] + f[count - a] for a in range(1, half)}
        minus = {a: f[a] - f[count - a] for a in range(1, half)}
        for j in range(count + 1):
            for_cos, for_sin = (plus, minus) if j % 2 == 0 else (minus, plus)
            angle = [math.pi * a * j / count for a in range(count)]
            real = weighted(
                [(1.0, f[0]), (math.cos(angle[half]), f[half])]
                + [(math.cos(angle[a]), for_cos[a]) for a in range(1, half)]
            )
            imag = weighted(
                [(-math.sin(angle[half]), f[half])]
                + [(-math.sin(angle[a]), for_sin[a]) for a in range(1, half)]
            )
            if imag is None:
                imag = jnp.zeros_like(real)
            for top, value in ((at, real), (pl.multiple_of(span + at, rows), imag)):
                high = value.astype(jnp.bfloat16)
                parts[j, pl.ds(top, rows), :cols] = high
                parts[j, pl.ds(top, rows), cols:] = (value - high.astype(jnp.float32)).astype(
                    jnp.bfloat16
                )


def split_dot(table, j, both, cols):
    main = jnp.dot(table[j, 0], both, preferred_element_type=jnp.float32)
    rest = jnp.dot(table[j, 1], both[:, :cols], preferred_element_type=jnp.float32)
    return main[:, :cols] + (main[:, cols:] + rest)


def fine_stage(parts, spectrum, there, back_table, back, own, arrive, pass_over, passed):
    half = back.shape[0] // 2
    span, cols = spectrum.shape[3], spectrum.shape[4]

    def one(k, b):
        j = 2 * b + k
        source = jnp.where(j <= half, j, 2 * half - j)
        full = split_dot(there, j, parts[source], cols)
        full_re, full_im = full[:span], full[span:]
        filt_re = spectrum[k, b, 0].astype(jnp.float32)
        filt_im = spectrum[k, b, 1].astype(jnp.float32)
        prod_re = filt_re * full_re - filt_im * full_im
        prod_im = filt_re * full_im + filt_im * full_re
        prod = jnp.concatenate([prod_re, prod_im], axis=0)
        high = prod.astype(jnp.bfloat16)
        low = (prod - high.astype(jnp.float32)).astype(jnp.bfloat16)
        both = jnp.concatenate([high, low], axis=1)
        back[j] = split_dot(back_table, j, both, cols)

    @pl.loop(0, half // 2)
    def _(v):
        blocks = arrive(v)
        for b in blocks:
            pass_over(b)
        for b in blocks:
            one(own, b)
        for b in blocks:
            passed(b)
        for b in blocks:
            one(1 - own, b)


def coarse_back(back, field, gate, skip, result, rows, first, last):
    count, span, cols = field.shape
    half = count // 2
    direct = jnp.broadcast_to(skip, (rows, cols))

    @pl.loop(first // rows, last // rows)
    def _(i):
        at = pl.multiple_of(i * rows, rows)
        low = pl.multiple_of(span + at, rows)

        def real(j):
            return back[j, pl.ds(at, rows), :]

        def imag(j):
            return back[j, pl.ds(low, rows), :]

        re = [real(0)] + [real(j) + real(2 * count - j) for j in range(1, count)] + [real(count)]
        im = [None] + [imag(j) - imag(2 * count - j) for j in range(1, count)] + [None]
        even_re = [re[j] + re[count - j] for j in range(half)]
        odd_re = [re[j] - re[count - j] for j in range(half)]
        even_im = [None] + [im[j] - im[count - j] for j in range(1, half)]
        odd_im = [None] + [im[j] + im[count - j] for j in range(1, half)]
        for a in range(count):
            use_re, use_im = (even_re, even_im) if a % 2 == 0 else (odd_re, odd_im)
            angle = [math.pi * a * j / count for j in range(half + 1)]
            total = weighted(
                [(math.cos(angle[j]), use_re[j]) for j in range(half)]
                + [(math.cos(angle[half]), re[half]), (-math.sin(angle[half]), im[half])]
                + [(-math.sin(angle[j]), use_im[j]) for j in range(1, half)]
            )
            values = field[a, pl.ds(at, rows), :].astype(jnp.float32)
            total = total + direct * values
            if gate is not None:
                total = gate[a, pl.ds(at, rows), :].astype(jnp.float32) * total
            result[a, pl.ds(at, rows), :] = total.astype(jnp.bfloat16)


def build_tables(tab, there, back_table, turn, count, span):
    turn[0] = tab[0]
    turn[1] = tab[1]
    turn[2] = tab[0]
    turn[3] = tab[1]
    scale = 1.0 / (2 * count * span)

    @pl.loop(0, 2 * count)
    def _(j):
        flip = jnp.where(j > count, -1.0, 1.0).astype(jnp.float32)
        cos_a, sin_a, cos_b, sin_b = turn[0], turn[1], turn[2], turn[3]
        cos_s, sin_s = cos_b * scale, sin_b * scale
        entries = (
            (there, cos_a, sin_a * flip, -sin_a, cos_a * flip),
            (back_table, cos_s, -sin_s, sin_s, cos_s),
        )
        places = ((0, 0), (0, 1), (1, 0), (1, 1))
        for table, *blocks in entries:
            for (row, col), value in zip(places, blocks):
                at = (slice(row * span, row * span + span), slice(col * span, col * span + span))
                high = value.astype(jnp.bfloat16)
                table[(j, 0) + at] = high
                table[(j, 1) + at] = (value - high.astype(jnp.float32)).astype(jnp.bfloat16)
        turn[0] = cos_a * tab[4] - sin_a * tab[5]
        turn[1] = sin_a * tab[4] + cos_a * tab[5]
        turn[2] = cos_b * tab[2] - sin_b * tab[3]
        turn[3] = sin_b * tab[2] + cos_b * tab[3]


def block_kernel(
    count,
    signal,
    gate_one,
    gate_two,
    spec_one,
    spec_two,
    skip_one,
    skip_two,
    weight,
    tab,
    out,
    in_signal,
    in_gate_one,
    in_gate_two,
    in_spec_one,
    in_spec_two,
    in_skip,
    there,
    back_table,
    turn,
    parts,
    back,
    second_field,
    mixed,
    arrived,
    features,
    totals,
    to_other,
    from_other,
    rows_all,
    send_sem,
    own_sem,
    recv_sem,
    spec_recv,
    relay_recv,
    weight_recv,
    mix_recv,
    pass_recv,
    other_recv,
    known_sem,
):
    g, s, m = lax.axis_index("grp"), lax.axis_index("seq"), lax.axis_index("mdl")
    span, cols = in_signal.shape[1], in_signal.shape[2]
    levels = count // 2
    z, x = s // 2, lax.rem(s, 2)
    above, below = z < levels - 1, z > 0
    beside_levels = jnp.where(above & below, 2, 1)

    def tell_levels(sem):
        @pl.when(above)
        def _():
            pl.semaphore_signal(sem, inc=1, device_id=(g, s + 2, m), device_id_type=MESH)

        @pl.when(below)
        def _():
            pl.semaphore_signal(sem, inc=1, device_id=(g, s - 2, m), device_id_type=MESH)

    barrier = pltpu.get_barrier_semaphore()
    tell_levels(barrier)

    @pl.loop(1, 8)
    def _(o):
        peer = lax.rem((g * 2 + x) * 2 + m + o, 8)
        pl.semaphore_signal(
            barrier,
            inc=1,
            device_id=(peer // 4, 2 * z + lax.rem(peer // 2, 2), lax.rem(peer, 2)),
            device_id_type=MESH,
        )

    pl.semaphore_wait(barrier, 7 + beside_levels)

    def hear_levels():
        @pl.loop(0, levels - 1)
        def _(r):
            tell_levels(known_sem.at[r])
            pl.semaphore_wait(known_sem.at[r], beside_levels)

    def level(v):
        return 2 * lax.rem(z // 2 + v // 2, 2) + lax.rem(z + v, 2)

    def columns(block):
        return pl.ds(pl.multiple_of(block * cols, cols), cols)

    def remote(source, target, send, recv, where):
        return pltpu.make_async_remote_copy(
            src_ref=source,
            dst_ref=target,
            send_sem=send,
            recv_sem=recv,
            device_id=where,
            device_id_type=MESH,
        )

    def local(source, target, recv):
        return pltpu.make_async_copy(source, target, recv)

    def take(view, sem):
        pltpu.make_async_copy(view, view, sem).wait()

    own_here = (g == m) & (x == m)

    def send_rows(array, buffer, slot):
        for v in (2, 3, 1, 0):
            to_z = level(v)
            for away in (1, 0):
                plane = g if away == 0 else 1 - g
                source = array.at[:, columns(2 * to_z + plane)]
                where = (plane, 2 * to_z + m, g)
                if v or away:
                    remote(
                        source, buffer.at[s], send_sem.at[slot], recv_sem.at[slot], where
                    ).start()
                    continue

                @pl.when(own_here)
                def _():
                    local(source, buffer.at[s], recv_sem.at[slot]).start()

                @pl.when(jnp.logical_not(own_here))
                def _():
                    remote(
                        source, buffer.at[s], own_sem.at[slot], recv_sem.at[slot], where
                    ).start()

    def send_spectrum(array, buffer, slot, which):
        for v in (2, 3, 1, 0):
            to_z = level(v)
            for other in (1, 0):
                k = 1 - m if other else m
                source = array.at[:, k, :, columns(2 * to_z + g)]
                target = buffer.at[k, s]
                recv = spec_recv.at[which, s]
                where = (g, 2 * to_z + m, k)
                if v or other:
                    remote(source, target, send_sem.at[slot], recv, where).start()
                    continue

                @pl.when(x == m)
                def _():
                    local(source, target, recv).start()

                @pl.when(x != m)
                def _():
                    remote(source, target, own_sem.at[slot], recv, where).start()

    def send_gate_two():
        for v in range(levels):
            source = gate_two.at[:, columns(2 * v + 1 - g)]
            target = in_gate_two.at[:, columns(levels * m + v)]
            remote(source, target, send_sem.at[4], recv_sem.at[4], (1 - g, s, g)).start()

            source = gate_two.at[:, columns(2 * v + g)]

            @pl.when(g == m)
            def _():
                local(source, target, recv_sem.at[4]).start()

            @pl.when(g != m)
            def _():
                remote(source, target, own_sem.at[4], recv_sem.at[4], (g, s, g)).start()

    def send_skips():
        @pl.when(x == m)
        def _():
            for at, skip in enumerate((skip_one, skip_two)):
                local(skip, in_skip.at[at], recv_sem.at[5]).start()
                remote(
                    skip, in_skip.at[at], own_sem.at[5], recv_sem.at[5], (g, s, 1 - m)
                ).start()

    depth = weight.shape[0] // 2
    pieces = weight_recv.shape[0]
    piece = depth // pieces
    beside = s + 1 - 2 * x

    def chunk(block, p):
        return rows_all.at[pl.ds(pl.multiple_of(block * depth + p * piece, piece), piece), :]

    def on_line(v):
        return 2 * level(v) + x

    def post(block, p, source, where, slot):
        remote(
            source, chunk(block, p), send_sem.at[11], weight_recv.at[p, slot], (g, where, m)
        ).start()

    def landed(block, p, slot):
        take(chunk(block, p), weight_recv.at[p, slot])

    def own_piece(p):
        return weight.at[pl.ds(pl.multiple_of(g * depth + p * piece, piece), piece), :]

    def weight_cross(p, inner):
        @pl.when((above & below) if inner else jnp.logical_not(above & below))
        def _():
            post(s, p, own_piece(p), on_line(3), 3)

    def weight_own(p):
        post(s, p, own_piece(p), on_line(1), 1)
        post(s, p, own_piece(p), beside, 4)
        local(own_piece(p), chunk(s, p), weight_recv.at[p, 0]).start()

    def weight_near(p):
        block = on_line(1)
        landed(block, p, 1)
        post(block, p, chunk(block, p), beside, 5)

    def weight_far(p):
        block = on_line(3)
        landed(block, p, 3)
        post(block, p, chunk(block, p), on_line(1), 2)
        post(block, p, chunk(block, p), beside, 7)

    def weight_last(p):
        block = on_line(2)
        landed(block, p, 2)
        post(block, p, chunk(block, p), beside, 6)

    def weight_end():
        for p in range(pieces):
            landed(s, p, 0)
            for v in range(levels):
                landed(2 * level(v) + 1 - x, p, 4 + v)

    def relay(buffer, which, b):
        return remote(
            buffer.at[m, b],
            buffer.at[m, b],
            send_sem.at[6 + which],
            relay_recv.at[which, b],
            (g, s, 1 - m),
        )

    def fine(buffer, which):
        def arrive(v):
            blocks = (2 * level(v) + x, 2 * level(v) + 1 - x)
            for b in blocks:
                take(buffer.at[m, b], spec_recv.at[which, b])
            return blocks

        def pass_over(b):
            relay(buffer, which, b).start()

        def passed(b):
            take(buffer.at[1 - m, b], relay_recv.at[which, b])

        fine_stage(parts, buffer, there, back_table, back, m, arrive, pass_over, passed)

    weight_cross(0, True)
    weight_cross(1, True)
    weight_own(0)
    weight_own(1)
    hear_levels()
    weight_cross(0, False)
    weight_cross(1, False)
    send_rows(signal, in_signal, 0)
    send_spectrum(spec_one, in_spec_one, 2, 0)
    build_tables(tab, there, back_table, turn, count, span)
    weight_near(0)
    weight_near(1)
    weight_far(0)
    weight_far(1)
    send_rows(gate_one, in_gate_one, 1)
    weight_last(0)
    weight_last(1)
    send_spectrum(spec_two, in_spec_two, 3, 1)
    send_gate_two()
    send_skips()
    take(in_signal, recv_sem.at[0])
    coarse_forward(in_signal, parts, 16)
    fine(in_spec_one, 0)
    take(in_gate_one, recv_sem.at[1])
    take(in_skip, recv_sem.at[5])
    mine = pl.ds(2 * z + g, 1)
    coarse_back(back, in_signal, in_gate_one, in_skip[0, mine, :], second_field, 16, 0, span)
    coarse_forward(second_field, parts, 16)
    fine(in_spec_two, 1)

    rows = span // mix_recv.shape[0]
    place = columns(levels * x + z)

    def strip(r):
        return pl.ds(r * rows, rows)

    mixes_other = m != g
    other, here = 1 - g, g

    def deliver(r):
        for v in (2, 3, 1, 0):
            for side in (0, 1):
                to = 2 * level(v) + (1 - x if side == 0 else x)
                source = mixed.at[to, strip(r), :]
                target = arrived.at[strip(r), place]
                if v or side == 0:
                    remote(source, target, send_sem.at[8], mix_recv.at[r], (g, to, m)).start()
                else:
                    local(source, target, mix_recv.at[r]).start()

    for r in range(span // rows):
        skip = in_skip[1, mine, :]
        coarse_back(back, second_field, None, skip, mixed, 16, r * rows, r * rows + rows)

        @pl.when(mixes_other)
        def _():
            deliver(r)

    take(in_gate_two, recv_sem.at[4])
    weight_end()

    def hand_over(r):
        view = features.at[m, strip(r), :]
        return remote(view, view, send_sem.at[9], pass_recv.at[r], (g, s, 1 - m))

    def exchange(r):
        source, target = to_other.at[strip(r), :], from_other.at[strip(r), :]
        return remote(source, target, send_sem.at[10], other_recv.at[r], (1 - g, s, m))

    def gate(r):
        take(arrived.at[strip(r), :], mix_recv.at[r])
        gated = in_gate_two[strip(r), :].astype(jnp.float32) * arrived[strip(r), :].astype(
            jnp.float32
        )
        features[m, strip(r), :] = gated.astype(jnp.bfloat16)
        hand_over(r).start()

    width = count * cols
    tile = 2 * cols

    def project(group, part, target):
        @pl.loop(0, width // tile)
        def _(i):
            at = pl.ds(pl.multiple_of(i * tile, tile), tile)
            sums = jnp.dot(
                features[group, part, :], rows_all[:, at], preferred_element_type=jnp.float32
            )
            target[part, at] = sums.astype(target.dtype)

    for r in range(span // rows):

        @pl.when(mixes_other)
        def _():
            gate(r)

        @pl.when(jnp.logical_not(mixes_other))
        def _():
            take(features.at[other, strip(r), :], pass_recv.at[r])
            if r == 0:
                for part in range(span // rows):
                    deliver(part)

        project(other, strip(r), to_other)
        exchange(r).start()

    for r in range(span // rows):

        @pl.when(jnp.logical_not(mixes_other))
        def _():
            gate(r)

        @pl.when(mixes_other)
        def _():
            take(features.at[here, strip(r), :], pass_recv.at[r])

    project(here, pl.ds(0, span), totals)

    for r in range(span // rows):
        take(from_other.at[strip(r), :], other_recv.at[r])
        more = from_other[strip(r), :].astype(jnp.float32)
        out[strip(r), :] = (totals[strip(r), :] + more).astype(out.dtype)

    most = pl.ds(0, count - 1)
    take(in_signal.at[most], send_sem.at[0])
    take(in_signal.at[most], send_sem.at[1])
    for which in range(2):
        take(in_spec_one.at[0, most], send_sem.at[2 + which])
        take(in_spec_one.at[0], send_sem.at[6 + which])
    half_gate = in_gate_two.at[:, pl.ds(0, width // 2)]
    take(half_gate, send_sem.at[4])
    take(in_signal.at[most], send_sem.at[8])
    take(arrived, send_sem.at[9])
    take(arrived, send_sem.at[10])
    take(rows_all.at[pl.ds(0, 7 * depth), :], send_sem.at[11])

    @pl.when(jnp.logical_not(own_here))
    def _():
        take(in_signal.at[0], own_sem.at[0])
        take(in_signal.at[0], own_sem.at[1])

    @pl.when(x != m)
    def _():
        take(in_spec_one.at[0, 0], own_sem.at[2])
        take(in_spec_one.at[0, 0], own_sem.at[3])

    @pl.when(x == m)
    def _():
        take(in_skip, own_sem.at[5])

    @pl.when(g != m)
    def _():
        take(half_gate, own_sem.at[4])


def direct_shards(
    signal,
    gate_first,
    gate_second,
    spectrum_first,
    spectrum_second,
    skip_first,
    skip_second,
    out_weight,
):
    count = lax.axis_size("seq")
    span, width = signal.shape
    cols = width // count
    coarse = 2 * count
    strips = 4
    anywhere = pl.BlockSpec(memory_space=pltpu.HBM)
    vmem = pl.BlockSpec(memory_space=pltpu.VMEM)
    bf16, f32 = jnp.bfloat16, jnp.float32
    return pl.pallas_call(
        functools.partial(block_kernel, count),
        out_shape=jax.ShapeDtypeStruct((span, width), bf16),
        in_specs=[anywhere] * 8 + [vmem],
        out_specs=vmem,
        scratch_shapes=[
            pltpu.VMEM((count, span, cols), bf16),
            pltpu.VMEM((count, span, cols), bf16),
            pltpu.VMEM((span, width), bf16),
            pltpu.VMEM((2, count, 2, span, cols), bf16),
            pltpu.VMEM((2, count, 2, span, cols), bf16),
            pltpu.VMEM((2, count, cols), f32),
            pltpu.VMEM((coarse, 2, 2 * span, 2 * span), bf16),
            pltpu.VMEM((coarse, 2, 2 * span, 2 * span), bf16),
            pltpu.VMEM((4, span, span), f32),
            pltpu.VMEM((count + 1, 2 * span, 2 * cols), bf16),
            pltpu.VMEM((coarse, 2 * span, cols), f32),
            pltpu.VMEM((count, span, cols), bf16),
            pltpu.VMEM((count, span, cols), bf16),
            pltpu.VMEM((span, width), bf16),
            pltpu.VMEM((2, span, width), bf16),
            pltpu.VMEM((span, width), f32),
            pltpu.VMEM((span, width), bf16),
            pltpu.VMEM((span, width), bf16),
            pltpu.VMEM((width, width), bf16),
            pltpu.SemaphoreType.DMA((12,)),
            pltpu.SemaphoreType.DMA((6,)),
            pltpu.SemaphoreType.DMA((6,)),
            pltpu.SemaphoreType.DMA((2, count)),
            pltpu.SemaphoreType.DMA((2, count)),
            pltpu.SemaphoreType.DMA((2, count)),
            pltpu.SemaphoreType.DMA((strips,)),
            pltpu.SemaphoreType.DMA((strips,)),
            pltpu.SemaphoreType.DMA((strips,)),
            pltpu.SemaphoreType.REGULAR((count // 2 - 1,)),
        ],
        compiler_params=pltpu.CompilerParams(
            collective_id=0, has_side_effects=True, vmem_limit_bytes=62 * 1024 * 1024
        ),
        cost_estimate=pl.CostEstimate(
            flops=16 * coarse * span * span * cols, bytes_accessed=1 << 26, transcendentals=0
        ),
    )(
        signal,
        gate_first,
        gate_second,
        spectrum_first,
        spectrum_second,
        skip_first.reshape(count, cols),
        skip_second.reshape(count, cols),
        out_weight,
        jnp.asarray(turn_tables(span, coarse)),
    )


def shards(*arrays):
    count = lax.axis_size("seq")
    span, width = arrays[0].shape
    pairs = lax.axis_size("grp") == 2 and lax.axis_size("mdl") == 2
    whole_tiles = width == count * LANES and span == LANES and count == 8
    if pairs and whole_tiles and arrays[3].shape[1] == 2:
        return direct_shards(*arrays)
    return plain_shards(*arrays)


def solution(mesh):
    placed = (
        P(("grp", "seq"), "mdl"),
        P(("grp", "seq"), "mdl"),
        P(("grp", "seq"), "mdl"),
        P(None, "seq", None, "mdl"),
        P(None, "seq", None, "mdl"),
        P("mdl"),
        P("mdl"),
        P("seq", "mdl"),
    )
    return jax.shard_map(
        shards, mesh=mesh, in_specs=placed, out_specs=P(("grp", "seq"), "mdl"), check_vma=False
    )
```

```python
import functools
import math

import jax
import jax.numpy as jnp
import numpy as np
from jax import lax
from jax.experimental import pallas as pl
from jax.experimental.pallas import tpu as pltpu
from jax.sharding import PartitionSpec as P

MESH = pl.DeviceIdType.MESH
LANES = 128


def angle_grid(first, second, modulus):
    product = first[:, None] * second[None, :] % modulus
    angles = product.astype(jnp.float32) * (2.0 * math.pi / modulus)
    return (jnp.cos(angles), jnp.sin(angles))


def mixing(form, left, right):
    return jnp.einsum(form, left, right, precision=lax.Precision.HIGHEST)


def complex_mix(form, real_table, imag_table, values_re, values_im):
    first_term = mixing(form, real_table, values_re + values_im)
    second_term = mixing(form, real_table + imag_table, values_im)
    third_term = mixing(form, imag_table - real_table, values_re)
    return (first_term - second_term, first_term + third_term)


def channel_filter(field, spectrum):
    coarse = spectrum.shape[1]
    span = spectrum.shape[2]
    count = coarse // 2
    cols = field.shape[1]
    length = coarse * span
    pencil = field.reshape(count, span, cols)
    coarse_ids = jnp.arange(coarse, dtype=jnp.int32)
    cos_a, sin_a = angle_grid(coarse_ids, jnp.arange(count, dtype=jnp.int32), coarse)
    part_re = mixing("ka,amc->kmc", cos_a, pencil)
    part_im = -mixing("ka,amc->kmc", sin_a, pencil)
    fine_ids = jnp.arange(span, dtype=jnp.int32)
    cos_t, sin_t = angle_grid(coarse_ids, fine_ids, length)
    cos_t = cos_t[:, :, None]
    sin_t = sin_t[:, :, None]
    turned_re = part_re * cos_t + part_im * sin_t
    turned_im = part_im * cos_t - part_re * sin_t
    cos_s, sin_s = angle_grid(fine_ids, fine_ids, span)
    full_re, full_im = complex_mix("qm,kmc->kqc", cos_s, -sin_s, turned_re, turned_im)
    filt_re = spectrum[0].astype(jnp.float32)
    filt_im = spectrum[1].astype(jnp.float32)
    prod_re = filt_re * full_re - filt_im * full_im
    prod_im = filt_re * full_im + filt_im * full_re
    inner_re, inner_im = complex_mix("mq,kqc->kmc", cos_s, sin_s, prod_re, prod_im)
    back_re = inner_re * cos_t - inner_im * sin_t
    back_im = inner_im * cos_t + inner_re * sin_t
    result = mixing("ka,kmc->amc", cos_a, back_re) - mixing("ka,kmc->amc", sin_a, back_im)
    return (result / length).reshape(count * span, cols)


def plain_shards(
    signal,
    gate_first,
    gate_second,
    spectrum_first,
    spectrum_second,
    skip_first,
    skip_second,
    out_weight,
):
    seq_index = lax.axis_index("seq")
    width = signal.shape[1]
    parts_seq = lax.axis_size("seq")
    cols = width // parts_seq
    col_sig, col_first, col_second = (
        lax.all_to_all(signal, "seq", split_axis=1, concat_axis=0, tiled=True),
        lax.all_to_all(gate_first, "seq", split_axis=1, concat_axis=0, tiled=True),
        lax.all_to_all(gate_second, "seq", split_axis=1, concat_axis=0, tiled=True),
    )
    spec_one, spec_two = (
        lax.all_to_all(spectrum_first, "seq", split_axis=3, concat_axis=1, tiled=True),
        lax.all_to_all(spectrum_second, "seq", split_axis=3, concat_axis=1, tiled=True),
    )
    skip_one = lax.dynamic_slice_in_dim(skip_first, seq_index * cols, cols, 0)
    skip_two = lax.dynamic_slice_in_dim(skip_second, seq_index * cols, cols, 0)
    values = col_sig.astype(jnp.float32)
    first_conv = channel_filter(values, spec_one) + skip_one * values
    first_out = (col_first.astype(jnp.float32) * first_conv).astype(jnp.bfloat16)
    first_vals = first_out.astype(jnp.float32)
    second_conv = channel_filter(first_vals, spec_two) + skip_two * first_vals
    mixed_cols = (col_second.astype(jnp.float32) * second_conv).astype(jnp.bfloat16)
    mixed = lax.all_to_all(mixed_cols, "seq", split_axis=0, concat_axis=1, tiled=True)
    features = lax.all_gather(mixed, "mdl", axis=1, tiled=True)
    total = jnp.dot(
        features,
        lax.all_gather(out_weight, "seq", axis=0, tiled=True),
        preferred_element_type=jnp.float32,
    )
    return total.astype(jnp.bfloat16)


def turn_tables(span, coarse):
    ids = np.arange(span)
    fine = 2.0 * math.pi * (ids[:, None] * ids[None, :] % span) / span
    step = 2.0 * math.pi * np.broadcast_to(ids[:, None], (span, span)) / (span * coarse)
    return np.stack(
        [np.cos(fine), np.sin(fine), np.cos(step), np.sin(step), np.cos(step).T, np.sin(step).T]
    ).astype(np.float32)


def weighted(terms):
    total = None
    for weight, value in terms:
        if abs(weight) < 1e-12:
            continue
        if abs(weight - 1.0) < 1e-12:
            term = value
        elif abs(weight + 1.0) < 1e-12:
            total = -value if total is None else total - value
            continue
        else:
            term = value * weight
        total = term if total is None else total + term
    return total


def coarse_forward(field, parts, rows):
    count, span, cols = field.shape
    half = count // 2

    @pl.loop(0, span // rows)
    def _(i):
        at = pl.multiple_of(i * rows, rows)
        f = [field[a, pl.ds(at, rows), :].astype(jnp.float32) for a in range(count)]
        plus = {a: f[a] + f[count - a] for a in range(1, half)}
        minus = {a: f[a] - f[count - a] for a in range(1, half)}
        for j in range(count + 1):
            for_cos, for_sin = (plus, minus) if j % 2 == 0 else (minus, plus)
            angle = [math.pi * a * j / count for a in range(count)]
            real = weighted(
                [(1.0, f[0]), (math.cos(angle[half]), f[half])]
                + [(math.cos(angle[a]), for_cos[a]) for a in range(1, half)]
            )
            imag = weighted(
                [(-math.sin(angle[half]), f[half])]
                + [(-math.sin(angle[a]), for_sin[a]) for a in range(1, half)]
            )
            if imag is None:
                imag = jnp.zeros_like(real)
            for top, value in ((at, real), (pl.multiple_of(span + at, rows), imag)):
                high = value.astype(jnp.bfloat16)
                parts[j, pl.ds(top, rows), :cols] = high
                parts[j, pl.ds(top, rows), cols:] = (value - high.astype(jnp.float32)).astype(
                    jnp.bfloat16
                )


def split_dot(table, j, both, cols):
    main = jnp.dot(table[j, 0], both, preferred_element_type=jnp.float32)
    rest = jnp.dot(table[j, 1], both[:, :cols], preferred_element_type=jnp.float32)
    return main[:, :cols] + (main[:, cols:] + rest)


def fine_stage(parts, spectrum, there, back_table, back, own, arrive, pass_over, passed):
    half = back.shape[0] // 2
    span, cols = spectrum.shape[3], spectrum.shape[4]

    def one(k, b):
        j = 2 * b + k
        source = jnp.where(j <= half, j, 2 * half - j)
        full = split_dot(there, j, parts[source], cols)
        full_re, full_im = full[:span], full[span:]
        filt_re = spectrum[k, b, 0].astype(jnp.float32)
        filt_im = spectrum[k, b, 1].astype(jnp.float32)
        prod_re = filt_re * full_re - filt_im * full_im
        prod_im = filt_re * full_im + filt_im * full_re
        prod = jnp.concatenate([prod_re, prod_im], axis=0)
        high = prod.astype(jnp.bfloat16)
        low = (prod - high.astype(jnp.float32)).astype(jnp.bfloat16)
        both = jnp.concatenate([high, low], axis=1)
        back[j] = split_dot(back_table, j, both, cols)

    @pl.loop(0, half // 2)
    def _(v):
        blocks = arrive(v)
        for b in blocks:
            pass_over(b)
        for b in blocks:
            one(own, b)
        for b in blocks:
            passed(b)
        for b in blocks:
            one(1 - own, b)


def coarse_back(back, field, gate, skip, result, rows, first, last):
    count, span, cols = field.shape
    half = count // 2
    direct = jnp.broadcast_to(skip, (rows, cols))

    @pl.loop(first // rows, last // rows)
    def _(i):
        at = pl.multiple_of(i * rows, rows)
        low = pl.multiple_of(span + at, rows)

        def real(j):
            return back[j, pl.ds(at, rows), :]

        def imag(j):
            return back[j, pl.ds(low, rows), :]

        re = [real(0)] + [real(j) + real(2 * count - j) for j in range(1, count)] + [real(count)]
        im = [None] + [imag(j) - imag(2 * count - j) for j in range(1, count)] + [None]
        even_re = [re[j] + re[count - j] for j in range(half)]
        odd_re = [re[j] - re[count - j] for j in range(half)]
        even_im = [None] + [im[j] - im[count - j] for j in range(1, half)]
        odd_im = [None] + [im[j] + im[count - j] for j in range(1, half)]
        for a in range(count):
            use_re, use_im = (even_re, even_im) if a % 2 == 0 else (odd_re, odd_im)
            angle = [math.pi * a * j / count for j in range(half + 1)]
            total = weighted(
                [(math.cos(angle[j]), use_re[j]) for j in range(half)]
                + [(math.cos(angle[half]), re[half]), (-math.sin(angle[half]), im[half])]
                + [(-math.sin(angle[j]), use_im[j]) for j in range(1, half)]
            )
            values = field[a, pl.ds(at, rows), :].astype(jnp.float32)
            total = total + direct * values
            if gate is not None:
                total = gate[a, pl.ds(at, rows), :].astype(jnp.float32) * total
            result[a, pl.ds(at, rows), :] = total.astype(jnp.bfloat16)


def build_tables(tab, there, back_table, turn, count, span):
    turn[0] = tab[0]
    turn[1] = tab[1]
    turn[2] = tab[0]
    turn[3] = tab[1]
    scale = 1.0 / (2 * count * span)

    @pl.loop(0, 2 * count)
    def _(j):
        flip = jnp.where(j > count, -1.0, 1.0).astype(jnp.float32)
        cos_a, sin_a, cos_b, sin_b = turn[0], turn[1], turn[2], turn[3]
        cos_s, sin_s = cos_b * scale, sin_b * scale
        entries = (
            (there, cos_a, sin_a * flip, -sin_a, cos_a * flip),
            (back_table, cos_s, -sin_s, sin_s, cos_s),
        )
        places = ((0, 0), (0, 1), (1, 0), (1, 1))
        for table, *blocks in entries:
            for (row, col), value in zip(places, blocks):
                at = (slice(row * span, row * span + span), slice(col * span, col * span + span))
                high = value.astype(jnp.bfloat16)
                table[(j, 0) + at] = high
                table[(j, 1) + at] = (value - high.astype(jnp.float32)).astype(jnp.bfloat16)
        turn[0] = cos_a * tab[4] - sin_a * tab[5]
        turn[1] = sin_a * tab[4] + cos_a * tab[5]
        turn[2] = cos_b * tab[2] - sin_b * tab[3]
        turn[3] = sin_b * tab[2] + cos_b * tab[3]


def block_kernel(
    count,
    signal,
    gate_one,
    gate_two,
    spec_one,
    spec_two,
    skip_one,
    skip_two,
    weight,
    tab,
    out,
    in_signal,
    in_gate_one,
    in_gate_two,
    in_spec_one,
    in_spec_two,
    in_skip,
    there,
    back_table,
    turn,
    parts,
    back,
    second_field,
    mixed,
    arrived,
    features,
    totals,
    rows_all,
    send_sem,
    own_sem,
    recv_sem,
    spec_recv,
    relay_recv,
    weight_recv,
    plane_recv,
    whole_recv,
    known_sem,
    mix_recv,
    pass_recv,
):
    g, s, m = lax.axis_index("grp"), lax.axis_index("seq"), lax.axis_index("mdl")
    span, cols = in_signal.shape[1], in_signal.shape[2]
    levels = count // 2
    z, x = s // 2, lax.rem(s, 2)
    above, below = z < levels - 1, z > 0
    beside_levels = jnp.where(above & below, 2, 1)

    def tell_levels(sem):
        @pl.when(above)
        def _():
            pl.semaphore_signal(sem, inc=1, device_id=(g, s + 2, m), device_id_type=MESH)

        @pl.when(below)
        def _():
            pl.semaphore_signal(sem, inc=1, device_id=(g, s - 2, m), device_id_type=MESH)

    barrier = pltpu.get_barrier_semaphore()
    tell_levels(barrier)

    @pl.loop(1, 8)
    def _(o):
        peer = lax.rem((g * 2 + x) * 2 + m + o, 8)
        pl.semaphore_signal(
            barrier,
            inc=1,
            device_id=(peer // 4, 2 * z + lax.rem(peer // 2, 2), lax.rem(peer, 2)),
            device_id_type=MESH,
        )

    pl.semaphore_wait(barrier, 7 + beside_levels)

    def hear_levels():
        @pl.loop(0, levels - 1)
        def _(r):
            tell_levels(known_sem.at[r])
            pl.semaphore_wait(known_sem.at[r], beside_levels)

    def level(v):
        return 2 * lax.rem(z // 2 + v // 2, 2) + lax.rem(z + v, 2)

    def columns(block):
        return pl.ds(pl.multiple_of(block * cols, cols), cols)

    def remote(source, target, send, recv, where):
        return pltpu.make_async_remote_copy(
            src_ref=source,
            dst_ref=target,
            send_sem=send,
            recv_sem=recv,
            device_id=where,
            device_id_type=MESH,
        )

    def local(source, target, recv):
        return pltpu.make_async_copy(source, target, recv)

    def take(view, sem):
        pltpu.make_async_copy(view, view, sem).wait()

    def swap(source, target, slot):
        @pl.when(g == m)
        def _():
            local(source, target, recv_sem.at[slot]).start()

        @pl.when(g != m)
        def _():
            remote(source, target, own_sem.at[slot], recv_sem.at[slot], (m, s, g)).start()

    def others():
        for v in (2, 3, 1):
            for side in (1 - x, x):
                yield 2 * level(v) + side
        yield s + 1 - 2 * x

    def send_rows(array, buffer, slot):
        for c in others():
            remote(
                array.at[:, columns(c)],
                buffer.at[s],
                send_sem.at[slot],
                recv_sem.at[slot],
                (m, c, g),
            ).start()
        swap(array.at[:, columns(s)], buffer.at[s], slot)

    def send_spectrum(array, buffer, slot, which):
        recv = spec_recv.at[which, s]

        @pl.when(g == m)
        def _():
            for c in others():
                for k in range(2):
                    remote(
                        array.at[:, k, :, columns(c)],
                        buffer.at[k, s],
                        send_sem.at[slot],
                        recv,
                        (g, c, k),
                    ).start()
            source = array.at[:, 1 - m, :, columns(s)]
            remote(source, buffer.at[1 - m, s], send_sem.at[slot], recv, (g, s, 1 - m)).start()
            local(array.at[:, m, :, columns(s)], buffer.at[m, s], recv).start()

    beside = s + 1 - 2 * x
    depth = weight.shape[0]
    pieces = weight_recv.shape[0]
    piece = depth // 2 // pieces

    def chunk(block, p, half=None):
        at = block * depth + (g if half is None else half) * (depth // 2) + p * piece
        return rows_all.at[pl.ds(pl.multiple_of(at, piece), piece), :]

    def whole(block):
        return rows_all.at[pl.ds(pl.multiple_of(block * depth, depth), depth), :]

    def on_line(v):
        return 2 * level(v) + x

    def post(block, p, source, where, slot):
        remote(
            source, chunk(block, p), send_sem.at[7], weight_recv.at[p, slot], (g, where, m)
        ).start()

    def over(block, p):
        view = chunk(block, p)
        remote(view, view, own_sem.at[4], plane_recv.at[p, block], (1 - g, s, m)).start()

    def landed(block, p, slot):
        take(chunk(block, p), weight_recv.at[p, slot])

    def own_piece(p):
        at = g * (depth // 2) + p * piece
        return weight.at[pl.ds(pl.multiple_of(at, piece), piece), :]

    def weight_cross(inner):
        @pl.when((above & below) if inner else jnp.logical_not(above & below))
        def _():
            for p in range(pieces):
                post(s, p, own_piece(p), on_line(3), 3)

    def weight_own():
        for p in range(pieces):
            post(s, p, own_piece(p), on_line(1), 1)
        local(weight, whole(s), whole_recv.at[0]).start()

    def weight_beside():
        for p in range(pieces):
            post(s, p, own_piece(p), beside, 4)

    def weight_near(p):
        block = on_line(1)
        landed(block, p, 1)
        post(block, p, chunk(block, p), beside, 5)
        over(block, p)

    def weight_far(p):
        block = on_line(3)
        landed(block, p, 3)
        post(block, p, chunk(block, p), on_line(1), 2)
        post(block, p, chunk(block, p), beside, 7)
        over(block, p)

    def weight_last(p):
        block = on_line(2)
        landed(block, p, 2)
        post(block, p, chunk(block, p), beside, 6)
        over(block, p)

    def weight_side(p, v):
        block = 2 * level(v) + 1 - x
        landed(block, p, 4 + v)
        over(block, p)

    def weight_end():
        take(whole(s), whole_recv.at[0])
        for p in range(pieces):
            for v in range(levels):
                for side in (x, 1 - x)[v == 0 :]:
                    block = 2 * level(v) + side
                    take(chunk(block, p, 1 - g), plane_recv.at[p, block])

    def weight_sent():
        rows = rows_all.at[pl.ds(0, 7 * (depth // 2)), :]
        take(rows, send_sem.at[7])
        take(rows, own_sem.at[4])

    def relay(buffer, which, b):
        return remote(
            buffer.at[m, b],
            buffer.at[m, b],
            send_sem.at[5 + which],
            relay_recv.at[which, b],
            (g, s, 1 - m),
        )

    def fine(buffer, which):
        def arrive(v):
            blocks = (2 * level(v) + x, 2 * level(v) + 1 - x)
            for b in blocks:
                take(buffer.at[m, b], spec_recv.at[which, b])
            return blocks

        def pass_over(b):
            relay(buffer, which, b).start()

        def passed(b):
            take(buffer.at[1 - m, b], relay_recv.at[which, b])

        fine_stage(parts, buffer, there, back_table, back, m, arrive, pass_over, passed)

    own_gate = local(gate_two, in_gate_two, recv_sem.at[4])
    own_gate = local(gate_two, in_gate_two, recv_sem.at[4])
    weight_cross(True)
    weight_own()
    weight_beside()
    hear_levels()
    weight_cross(False)
    send_rows(signal, in_signal, 0)
    send_spectrum(spec_one, in_spec_one, 2, 0)
    build_tables(tab, there, back_table, turn, count, span)
    weight_near(0)
    weight_near(1)
    weight_far(0)
    weight_far(1)
    weight_side(0, 0)
    weight_side(1, 0)
    send_rows(gate_one, in_gate_one, 1)
    weight_last(0)
    weight_last(1)
    send_spectrum(spec_two, in_spec_two, 3, 1)
    own_gate.start()
    swap(skip_one, in_skip.at[0], 5)
    swap(skip_two, in_skip.at[1], 3)
    take(in_signal, recv_sem.at[0])
    coarse_forward(in_signal, parts, 16)
    weight_side(0, 1)
    weight_side(1, 1)
    fine(in_spec_one, 0)
    weight_side(0, 3)
    weight_side(1, 3)
    take(in_gate_one, recv_sem.at[1])
    take(in_skip.at[0], recv_sem.at[5])
    take(in_skip.at[1], recv_sem.at[3])
    mine = pl.ds(s, 1)
    coarse_back(back, in_signal, in_gate_one, in_skip[0, mine, :], second_field, 16, 0, span)
    coarse_forward(second_field, parts, 16)
    weight_side(0, 2)
    weight_side(1, 2)
    fine(in_spec_two, 1)

    rows = span // mix_recv.shape[0]

    def strip(r):
        return pl.ds(r * rows, rows)

    def deliver(c, r, own):
        return remote(
            mixed.at[c, strip(r), :],
            arrived.at[strip(r), columns(s)],
            own_sem.at[2] if own else send_sem.at[8],
            mix_recv.at[r],
            (m, c, g),
        )

    for r in range(span // rows):
        skip = in_skip[1, mine, :]
        coarse_back(back, second_field, None, skip, mixed, 16, r * rows, r * rows + rows)
        for c in others():
            deliver(c, r, False).start()

        @pl.when(g == m)
        def _():
            local(
                mixed.at[s, strip(r), :], arrived.at[strip(r), columns(s)], mix_recv.at[r]
            ).start()

        @pl.when(g != m)
        def _():
            deliver(s, r, True).start()

    own_gate.wait()
    weight_end()

    def hand_over(r):
        view = features.at[m, strip(r), :]
        return remote(view, view, send_sem.at[9], pass_recv.at[r], (g, s, 1 - m))

    width = count * cols
    tile = 2 * cols
    for r in range(span // rows):
        take(arrived.at[strip(r), :], mix_recv.at[r])
        gated = in_gate_two[strip(r), :].astype(jnp.float32) * arrived[strip(r), :].astype(
            jnp.float32
        )
        features[m, strip(r), :] = gated.astype(jnp.bfloat16)
        hand_over(r).start()

    def project(half, at):
        return jnp.dot(
            features[half],
            rows_all[pl.ds(pl.multiple_of(half * width, width), width), at],
            preferred_element_type=jnp.float32,
        )

    @pl.loop(0, width // tile)
    def _(i):
        at = pl.ds(pl.multiple_of(i * tile, tile), tile)
        totals[:, at] = project(m, at)

    for r in range(span // rows):
        take(features.at[1 - m, strip(r), :], pass_recv.at[r])

    @pl.loop(0, width // tile)
    def _(i):
        at = pl.ds(pl.multiple_of(i * tile, tile), tile)
        out[:, at] = (totals[:, at] + project(1 - m, at)).astype(out.dtype)

    weight_sent()

    most = pl.ds(0, count - 1)
    for slot in (0, 1, 8):
        take(in_signal.at[most], send_sem.at[slot])
    for which in range(2):
        take(in_spec_one.at[0], send_sem.at[5 + which])
    take(arrived, send_sem.at[9])

    @pl.when(g == m)
    def _():
        for which in range(2):
            take(in_spec_one.at[:, most], send_sem.at[2 + which])
            take(in_spec_one.at[0, 0], send_sem.at[2 + which])

    @pl.when(g != m)
    def _():
        for slot in (0, 1, 2):
            take(in_signal.at[0], own_sem.at[slot])
        take(in_skip.at[0], own_sem.at[5])
        take(in_skip.at[1], own_sem.at[3])


def direct_shards(
    signal,
    gate_first,
    gate_second,
    spectrum_first,
    spectrum_second,
    skip_first,
    skip_second,
    out_weight,
):
    count = lax.axis_size("seq")
    span, width = signal.shape
    cols = width // count
    coarse = 2 * count
    strips = 2
    anywhere = pl.BlockSpec(memory_space=pltpu.HBM)
    vmem = pl.BlockSpec(memory_space=pltpu.VMEM)
    bf16, f32 = jnp.bfloat16, jnp.float32
    return pl.pallas_call(
        functools.partial(block_kernel, count),
        out_shape=jax.ShapeDtypeStruct((span, width), bf16),
        in_specs=[anywhere] * 8 + [vmem],
        out_specs=vmem,
        scratch_shapes=[
            pltpu.VMEM((count, span, cols), bf16),
            pltpu.VMEM((count, span, cols), bf16),
            pltpu.VMEM((span, width), bf16),
            pltpu.VMEM((2, count, 2, span, cols), bf16),
            pltpu.VMEM((2, count, 2, span, cols), bf16),
            pltpu.VMEM((2, count, cols), f32),
            pltpu.VMEM((coarse, 2, 2 * span, 2 * span), bf16),
            pltpu.VMEM((coarse, 2, 2 * span, 2 * span), bf16),
            pltpu.VMEM((4, span, span), f32),
            pltpu.VMEM((count + 1, 2 * span, 2 * cols), bf16),
            pltpu.VMEM((coarse, 2 * span, cols), f32),
            pltpu.VMEM((count, span, cols), bf16),
            pltpu.VMEM((count, span, cols), bf16),
            pltpu.VMEM((span, width), bf16),
            pltpu.VMEM((2, span, width), bf16),
            pltpu.VMEM((span, width), f32),
            pltpu.VMEM((2 * width, width), bf16),
            pltpu.SemaphoreType.DMA((10,)),
            pltpu.SemaphoreType.DMA((6,)),
            pltpu.SemaphoreType.DMA((6,)),
            pltpu.SemaphoreType.DMA((2, count)),
            pltpu.SemaphoreType.DMA((2, count)),
            pltpu.SemaphoreType.DMA((2, count)),
            pltpu.SemaphoreType.DMA((2, count)),
            pltpu.SemaphoreType.DMA((1,)),
            pltpu.SemaphoreType.REGULAR((count // 2 - 1,)),
            pltpu.SemaphoreType.DMA((strips,)),
            pltpu.SemaphoreType.DMA((strips,)),
        ],
        compiler_params=pltpu.CompilerParams(
            collective_id=0, has_side_effects=True, vmem_limit_bytes=62 * 1024 * 1024
        ),
        cost_estimate=pl.CostEstimate(
            flops=16 * coarse * span * span * cols, bytes_accessed=1 << 26, transcendentals=0
        ),
    )(
        signal,
        gate_first,
        gate_second,
        spectrum_first,
        spectrum_second,
        skip_first.reshape(count, cols),
        skip_second.reshape(count, cols),
        out_weight,
        jnp.asarray(turn_tables(span, coarse)),
    )


def shards(*arrays):
    count = lax.axis_size("seq")
    span, width = arrays[0].shape
    pairs = lax.axis_size("grp") == 2 and lax.axis_size("mdl") == 2
    whole_tiles = width == count * LANES and span == LANES and count == 8
    if pairs and whole_tiles and arrays[3].shape[1] == 2:
        return direct_shards(*arrays)
    return plain_shards(*arrays)


def solution(mesh):
    placed = (
        P(("grp", "seq"), "mdl"),
        P(("grp", "seq"), "mdl"),
        P(("grp", "seq"), "mdl"),
        P(None, "seq", None, "mdl"),
        P(None, "seq", None, "mdl"),
        P("mdl"),
        P("mdl"),
        P("seq", "mdl"),
    )
    return jax.shard_map(
        shards, mesh=mesh, in_specs=placed, out_specs=P(("grp", "seq"), "mdl"), check_vma=False
    )
```

```python
import functools
import math

import jax
import jax.numpy as jnp
import numpy as np
from jax import lax
from jax.experimental import pallas as pl
from jax.experimental.pallas import tpu as pltpu
from jax.sharding import PartitionSpec as P

MESH = pl.DeviceIdType.MESH
LANES = 128


def angle_grid(first, second, modulus):
    product = first[:, None] * second[None, :] % modulus
    angles = product.astype(jnp.float32) * (2.0 * math.pi / modulus)
    return (jnp.cos(angles), jnp.sin(angles))


def mixing(form, left, right):
    return jnp.einsum(form, left, right, precision=lax.Precision.HIGHEST)


def complex_mix(form, real_table, imag_table, values_re, values_im):
    first_term = mixing(form, real_table, values_re + values_im)
    second_term = mixing(form, real_table + imag_table, values_im)
    third_term = mixing(form, imag_table - real_table, values_re)
    return (first_term - second_term, first_term + third_term)


def channel_filter(field, spectrum):
    coarse = spectrum.shape[1]
    span = spectrum.shape[2]
    count = coarse // 2
    cols = field.shape[1]
    length = coarse * span
    pencil = field.reshape(count, span, cols)
    coarse_ids = jnp.arange(coarse, dtype=jnp.int32)
    cos_a, sin_a = angle_grid(coarse_ids, jnp.arange(count, dtype=jnp.int32), coarse)
    part_re = mixing("ka,amc->kmc", cos_a, pencil)
    part_im = -mixing("ka,amc->kmc", sin_a, pencil)
    fine_ids = jnp.arange(span, dtype=jnp.int32)
    cos_t, sin_t = angle_grid(coarse_ids, fine_ids, length)
    cos_t = cos_t[:, :, None]
    sin_t = sin_t[:, :, None]
    turned_re = part_re * cos_t + part_im * sin_t
    turned_im = part_im * cos_t - part_re * sin_t
    cos_s, sin_s = angle_grid(fine_ids, fine_ids, span)
    full_re, full_im = complex_mix("qm,kmc->kqc", cos_s, -sin_s, turned_re, turned_im)
    filt_re = spectrum[0].astype(jnp.float32)
    filt_im = spectrum[1].astype(jnp.float32)
    prod_re = filt_re * full_re - filt_im * full_im
    prod_im = filt_re * full_im + filt_im * full_re
    inner_re, inner_im = complex_mix("mq,kqc->kmc", cos_s, sin_s, prod_re, prod_im)
    back_re = inner_re * cos_t - inner_im * sin_t
    back_im = inner_im * cos_t + inner_re * sin_t
    result = mixing("ka,kmc->amc", cos_a, back_re) - mixing("ka,kmc->amc", sin_a, back_im)
    return (result / length).reshape(count * span, cols)


def plain_shards(
    signal,
    gate_first,
    gate_second,
    spectrum_first,
    spectrum_second,
    skip_first,
    skip_second,
    out_weight,
):
    seq_index = lax.axis_index("seq")
    width = signal.shape[1]
    parts_seq = lax.axis_size("seq")
    cols = width // parts_seq
    col_sig, col_first, col_second = (
        lax.all_to_all(signal, "seq", split_axis=1, concat_axis=0, tiled=True),
        lax.all_to_all(gate_first, "seq", split_axis=1, concat_axis=0, tiled=True),
        lax.all_to_all(gate_second, "seq", split_axis=1, concat_axis=0, tiled=True),
    )
    spec_one, spec_two = (
        lax.all_to_all(spectrum_first, "seq", split_axis=3, concat_axis=1, tiled=True),
        lax.all_to_all(spectrum_second, "seq", split_axis=3, concat_axis=1, tiled=True),
    )
    skip_one = lax.dynamic_slice_in_dim(skip_first, seq_index * cols, cols, 0)
    skip_two = lax.dynamic_slice_in_dim(skip_second, seq_index * cols, cols, 0)
    values = col_sig.astype(jnp.float32)
    first_conv = channel_filter(values, spec_one) + skip_one * values
    first_out = (col_first.astype(jnp.float32) * first_conv).astype(jnp.bfloat16)
    first_vals = first_out.astype(jnp.float32)
    second_conv = channel_filter(first_vals, spec_two) + skip_two * first_vals
    mixed_cols = (col_second.astype(jnp.float32) * second_conv).astype(jnp.bfloat16)
    mixed = lax.all_to_all(mixed_cols, "seq", split_axis=0, concat_axis=1, tiled=True)
    features = lax.all_gather(mixed, "mdl", axis=1, tiled=True)
    total = jnp.dot(
        features,
        lax.all_gather(out_weight, "seq", axis=0, tiled=True),
        preferred_element_type=jnp.float32,
    )
    return total.astype(jnp.bfloat16)


def turn_tables(span, coarse):
    ids = np.arange(span)
    fine = 2.0 * math.pi * (ids[:, None] * ids[None, :] % span) / span
    step = 2.0 * math.pi * np.broadcast_to(ids[:, None], (span, span)) / (span * coarse)
    return np.stack(
        [np.cos(fine), np.sin(fine), np.cos(step), np.sin(step), np.cos(step).T, np.sin(step).T]
    ).astype(np.float32)


def weighted(terms):
    total = None
    for weight, value in terms:
        if abs(weight) < 1e-12:
            continue
        if abs(weight - 1.0) < 1e-12:
            term = value
        elif abs(weight + 1.0) < 1e-12:
            total = -value if total is None else total - value
            continue
        else:
            term = value * weight
        total = term if total is None else total + term
    return total


def coarse_forward(field, parts, rows):
    count, span, cols = field.shape
    half = count // 2

    @pl.loop(0, span // rows)
    def _(i):
        at = pl.multiple_of(i * rows, rows)
        f = [field[a, pl.ds(at, rows), :].astype(jnp.float32) for a in range(count)]
        plus = {a: f[a] + f[count - a] for a in range(1, half)}
        minus = {a: f[a] - f[count - a] for a in range(1, half)}
        for j in range(count + 1):
            for_cos, for_sin = (plus, minus) if j % 2 == 0 else (minus, plus)
            angle = [math.pi * a * j / count for a in range(count)]
            real = weighted(
                [(1.0, f[0]), (math.cos(angle[half]), f[half])]
                + [(math.cos(angle[a]), for_cos[a]) for a in range(1, half)]
            )
            imag = weighted(
                [(-math.sin(angle[half]), f[half])]
                + [(-math.sin(angle[a]), for_sin[a]) for a in range(1, half)]
            )
            if imag is None:
                imag = jnp.zeros_like(real)
            for top, value in ((at, real), (pl.multiple_of(span + at, rows), imag)):
                high = value.astype(jnp.bfloat16)
                parts[j, pl.ds(top, rows), :cols] = high
                parts[j, pl.ds(top, rows), cols:] = (value - high.astype(jnp.float32)).astype(
                    jnp.bfloat16
                )


def split_dot(table, j, both, cols):
    main = jnp.dot(table[j, 0], both, preferred_element_type=jnp.float32)
    rest = jnp.dot(table[j, 1], both[:, :cols], preferred_element_type=jnp.float32)
    return main[:, :cols] + (main[:, cols:] + rest)


def fine_stage(parts, spectrum, there, back_table, back, own, arrive, pass_over, passed):
    half = back.shape[0] // 2
    span, cols = spectrum.shape[3], spectrum.shape[4]

    def one(k, b):
        j = 2 * b + k
        source = jnp.where(j <= half, j, 2 * half - j)
        full = split_dot(there, j, parts[source], cols)
        full_re, full_im = full[:span], full[span:]
        filt_re = spectrum[k, b, 0].astype(jnp.float32)
        filt_im = spectrum[k, b, 1].astype(jnp.float32)
        prod_re = filt_re * full_re - filt_im * full_im
        prod_im = filt_re * full_im + filt_im * full_re
        prod = jnp.concatenate([prod_re, prod_im], axis=0)
        high = prod.astype(jnp.bfloat16)
        low = (prod - high.astype(jnp.float32)).astype(jnp.bfloat16)
        both = jnp.concatenate([high, low], axis=1)
        back[j] = split_dot(back_table, j, both, cols)

    @pl.loop(0, half // 2)
    def _(v):
        blocks = arrive(v)
        for b in blocks:
            pass_over(b)
        for b in blocks:
            one(own, b)
        for b in blocks:
            passed(b)
        for b in blocks:
            one(1 - own, b)


def coarse_back(back, field, gate, skip, result, rows, first, last):
    count, span, cols = field.shape
    half = count // 2
    direct = jnp.broadcast_to(skip, (rows, cols))

    @pl.loop(first // rows, last // rows)
    def _(i):
        at = pl.multiple_of(i * rows, rows)
        low = pl.multiple_of(span + at, rows)

        def real(j):
            return back[j, pl.ds(at, rows), :]

        def imag(j):
            return back[j, pl.ds(low, rows), :]

        re = [real(0)] + [real(j) + real(2 * count - j) for j in range(1, count)] + [real(count)]
        im = [None] + [imag(j) - imag(2 * count - j) for j in range(1, count)] + [None]
        even_re = [re[j] + re[count - j] for j in range(half)]
        odd_re = [re[j] - re[count - j] for j in range(half)]
        even_im = [None] + [im[j] - im[count - j] for j in range(1, half)]
        odd_im = [None] + [im[j] + im[count - j] for j in range(1, half)]
        for a in range(count):
            use_re, use_im = (even_re, even_im) if a % 2 == 0 else (odd_re, odd_im)
            angle = [math.pi * a * j / count for j in range(half + 1)]
            total = weighted(
                [(math.cos(angle[j]), use_re[j]) for j in range(half)]
                + [(math.cos(angle[half]), re[half]), (-math.sin(angle[half]), im[half])]
                + [(-math.sin(angle[j]), use_im[j]) for j in range(1, half)]
            )
            values = field[a, pl.ds(at, rows), :].astype(jnp.float32)
            total = total + direct * values
            if gate is not None:
                total = gate[a, pl.ds(at, rows), :].astype(jnp.float32) * total
            result[a, pl.ds(at, rows), :] = total.astype(jnp.bfloat16)


def build_tables(tab, there, back_table, turn, count, span):
    turn[0] = tab[0]
    turn[1] = tab[1]
    turn[2] = tab[0]
    turn[3] = tab[1]
    scale = 1.0 / (2 * count * span)

    @pl.loop(0, 2 * count)
    def _(j):
        flip = jnp.where(j > count, -1.0, 1.0).astype(jnp.float32)
        cos_a, sin_a, cos_b, sin_b = turn[0], turn[1], turn[2], turn[3]
        cos_s, sin_s = cos_b * scale, sin_b * scale
        entries = (
            (there, cos_a, sin_a * flip, -sin_a, cos_a * flip),
            (back_table, cos_s, -sin_s, sin_s, cos_s),
        )
        places = ((0, 0), (0, 1), (1, 0), (1, 1))
        for table, *blocks in entries:
            for (row, col), value in zip(places, blocks):
                at = (slice(row * span, row * span + span), slice(col * span, col * span + span))
                high = value.astype(jnp.bfloat16)
                table[(j, 0) + at] = high
                table[(j, 1) + at] = (value - high.astype(jnp.float32)).astype(jnp.bfloat16)
        turn[0] = cos_a * tab[4] - sin_a * tab[5]
        turn[1] = sin_a * tab[4] + cos_a * tab[5]
        turn[2] = cos_b * tab[2] - sin_b * tab[3]
        turn[3] = sin_b * tab[2] + cos_b * tab[3]


def block_kernel(
    count,
    signal,
    gate_one,
    gate_two,
    spec_one,
    spec_two,
    skip_one,
    skip_two,
    weight,
    tab,
    out,
    in_signal,
    in_gate_one,
    in_gate_two,
    in_spec_one,
    in_spec_two,
    in_skip,
    there,
    back_table,
    turn,
    parts,
    back,
    second_field,
    mixed,
    arrived,
    features,
    totals,
    rows_all,
    send_sem,
    own_sem,
    recv_sem,
    spec_recv,
    relay_recv,
    weight_recv,
    plane_recv,
    whole_recv,
    known_sem,
    mix_recv,
    pass_recv,
):
    g, s, m = lax.axis_index("grp"), lax.axis_index("seq"), lax.axis_index("mdl")
    span, cols = in_signal.shape[1], in_signal.shape[2]
    levels = count // 2
    z, x = s // 2, lax.rem(s, 2)
    above, below = z < levels - 1, z > 0
    beside_levels = jnp.where(above & below, 2, 1)

    def tell_levels(sem):
        @pl.when(above)
        def _():
            pl.semaphore_signal(sem, inc=1, device_id=(g, s + 2, m), device_id_type=MESH)

        @pl.when(below)
        def _():
            pl.semaphore_signal(sem, inc=1, device_id=(g, s - 2, m), device_id_type=MESH)

    barrier = pltpu.get_barrier_semaphore()
    tell_levels(barrier)

    @pl.loop(1, 8)
    def _(o):
        peer = lax.rem((g * 2 + x) * 2 + m + o, 8)
        pl.semaphore_signal(
            barrier,
            inc=1,
            device_id=(peer // 4, 2 * z + lax.rem(peer // 2, 2), lax.rem(peer, 2)),
            device_id_type=MESH,
        )

    pl.semaphore_wait(barrier, 7 + beside_levels)

    def hear_levels():
        @pl.loop(0, levels - 1)
        def _(r):
            tell_levels(known_sem.at[r])
            pl.semaphore_wait(known_sem.at[r], beside_levels)

    def level(v):
        return 2 * lax.rem(z // 2 + v // 2, 2) + lax.rem(z + v, 2)

    def columns(block):
        return pl.ds(pl.multiple_of(block * cols, cols), cols)

    def remote(source, target, send, recv, where):
        return pltpu.make_async_remote_copy(
            src_ref=source,
            dst_ref=target,
            send_sem=send,
            recv_sem=recv,
            device_id=where,
            device_id_type=MESH,
        )

    def local(source, target, recv):
        return pltpu.make_async_copy(source, target, recv)

    def take(view, sem):
        pltpu.make_async_copy(view, view, sem).wait()

    def swap(source, target, slot):
        @pl.when(g == m)
        def _():
            local(source, target, recv_sem.at[slot]).start()

        @pl.when(g != m)
        def _():
            remote(source, target, own_sem.at[slot], recv_sem.at[slot], (m, s, g)).start()

    def others():
        for v in (2, 3, 1):
            for side in (1 - x, x):
                yield 2 * level(v) + side
        yield s + 1 - 2 * x

    def send_rows(array, buffer, slot):
        for c in others():
            remote(
                array.at[:, columns(c)],
                buffer.at[s],
                send_sem.at[slot],
                recv_sem.at[slot],
                (m, c, g),
            ).start()
        swap(array.at[:, columns(s)], buffer.at[s], slot)

    def send_spectrum(array, buffer, slot, which):
        recv = spec_recv.at[which, s]

        @pl.when(g == m)
        def _():
            for c in others():
                for k in range(2):
                    remote(
                        array.at[:, k, :, columns(c)],
                        buffer.at[k, s],
                        send_sem.at[slot],
                        recv,
                        (g, c, k),
                    ).start()
            source = array.at[:, 1 - m, :, columns(s)]
            remote(source, buffer.at[1 - m, s], send_sem.at[slot], recv, (g, s, 1 - m)).start()
            local(array.at[:, m, :, columns(s)], buffer.at[m, s], recv).start()

    beside = s + 1 - 2 * x
    depth = weight.shape[0]
    pieces = weight_recv.shape[0]
    piece = depth // 2 // pieces

    def chunk(block, p, half=None):
        at = block * depth + (g if half is None else half) * (depth // 2) + p * piece
        return rows_all.at[pl.ds(pl.multiple_of(at, piece), piece), :]

    def whole(block):
        return rows_all.at[pl.ds(pl.multiple_of(block * depth, depth), depth), :]

    def on_line(v):
        return 2 * level(v) + x

    def post(block, p, source, where, slot):
        remote(
            source, chunk(block, p), send_sem.at[7], weight_recv.at[p, slot], (g, where, m)
        ).start()

    def over(block, p):
        view = chunk(block, p)
        remote(view, view, own_sem.at[4], plane_recv.at[p, block], (1 - g, s, m)).start()

    def landed(block, p, slot):
        take(chunk(block, p), weight_recv.at[p, slot])

    def own_piece(p):
        at = g * (depth // 2) + p * piece
        return weight.at[pl.ds(pl.multiple_of(at, piece), piece), :]

    def weight_cross(inner):
        @pl.when((above & below) if inner else jnp.logical_not(above & below))
        def _():
            for p in range(pieces):
                post(s, p, own_piece(p), on_line(3), 3)

    def weight_own():
        for p in range(pieces):
            post(s, p, own_piece(p), on_line(1), 1)
        local(weight, whole(s), whole_recv.at[0]).start()

    def weight_beside():
        for p in range(pieces):
            post(s, p, own_piece(p), beside, 4)

    def weight_near(p):
        block = on_line(1)
        landed(block, p, 1)
        post(block, p, chunk(block, p), beside, 5)
        over(block, p)

    def weight_far(p):
        block = on_line(3)
        landed(block, p, 3)
        post(block, p, chunk(block, p), on_line(1), 2)
        post(block, p, chunk(block, p), beside, 7)
        over(block, p)

    def weight_last(p):
        block = on_line(2)
        landed(block, p, 2)
        post(block, p, chunk(block, p), beside, 6)
        over(block, p)

    def weight_side(p, v):
        block = 2 * level(v) + 1 - x
        landed(block, p, 4 + v)
        over(block, p)

    def weight_end():
        take(whole(s), whole_recv.at[0])
        for p in range(pieces):
            for v in range(levels):
                for side in (x, 1 - x)[v == 0 :]:
                    block = 2 * level(v) + side
                    take(chunk(block, p, 1 - g), plane_recv.at[p, block])

    def weight_sent():
        rows = rows_all.at[pl.ds(0, 7 * (depth // 2)), :]
        take(rows, send_sem.at[7])
        take(rows, own_sem.at[4])

    def relay(buffer, which, b):
        return remote(
            buffer.at[m, b],
            buffer.at[m, b],
            send_sem.at[5 + which],
            relay_recv.at[which, b],
            (g, s, 1 - m),
        )

    def fine(buffer, which):
        def arrive(v):
            blocks = (2 * level(v) + x, 2 * level(v) + 1 - x)
            for b in blocks:
                take(buffer.at[m, b], spec_recv.at[which, b])
            return blocks

        def pass_over(b):
            relay(buffer, which, b).start()

        def passed(b):
            take(buffer.at[1 - m, b], relay_recv.at[which, b])

        fine_stage(parts, buffer, there, back_table, back, m, arrive, pass_over, passed)

    own_gate = local(gate_two, in_gate_two, recv_sem.at[4])
    own_gate = local(gate_two, in_gate_two, recv_sem.at[4])
    weight_cross(True)
    weight_own()
    weight_beside()
    hear_levels()
    weight_cross(False)
    send_rows(signal, in_signal, 0)
    send_spectrum(spec_one, in_spec_one, 2, 0)
    build_tables(tab, there, back_table, turn, count, span)
    weight_near(0)
    weight_near(1)
    weight_side(0, 0)
    weight_side(1, 0)
    weight_far(0)
    weight_far(1)
    send_rows(gate_one, in_gate_one, 1)
    send_spectrum(spec_two, in_spec_two, 3, 1)
    weight_last(0)
    weight_last(1)
    own_gate.start()
    swap(skip_one, in_skip.at[0], 5)
    swap(skip_two, in_skip.at[1], 3)
    take(in_signal, recv_sem.at[0])
    coarse_forward(in_signal, parts, 16)
    weight_side(0, 1)
    weight_side(1, 1)
    fine(in_spec_one, 0)
    weight_side(0, 3)
    weight_side(1, 3)
    take(in_gate_one, recv_sem.at[1])
    take(in_skip.at[0], recv_sem.at[5])
    take(in_skip.at[1], recv_sem.at[3])
    mine = pl.ds(s, 1)
    coarse_back(back, in_signal, in_gate_one, in_skip[0, mine, :], second_field, 16, 0, span)
    coarse_forward(second_field, parts, 16)
    weight_side(0, 2)
    weight_side(1, 2)
    fine(in_spec_two, 1)

    skip = in_skip[1, mine, :]
    coarse_back(back, second_field, None, skip, mixed, 16, 0, span)

    width = count * cols
    tile = 2 * cols
    near, far = z // 2, 1 - z // 2

    def deliver(c, stage, own):
        return remote(
            mixed.at[c],
            arrived.at[:, columns(s)],
            own_sem.at[2] if own else send_sem.at[8],
            mix_recv.at[stage],
            (m, c, g),
        )

    for c, stage in zip(others(), (1, 1, 1, 1, 0, 0, 0)):
        deliver(c, stage, False).start()

    @pl.when(g == m)
    def _():
        local(mixed.at[s], arrived.at[:, columns(s)], mix_recv.at[0]).start()

    @pl.when(g != m)
    def _():
        deliver(s, 0, True).start()

    def part(side):
        return pl.ds(pl.multiple_of(side * (width // 2), width // 2), width // 2)

    def gate(side, stage):
        at = part(side)
        take(arrived.at[:, at], mix_recv.at[stage])
        gated = in_gate_two[:, at].astype(jnp.float32) * arrived[:, at].astype(jnp.float32)
        features[m, :, at] = gated.astype(jnp.bfloat16)
        view = features.at[m, :, at]
        remote(view, view, send_sem.at[9], pass_recv.at[stage], (g, s, 1 - m)).start()

    def passed(side, stage):
        take(features.at[1 - m, :, part(side)], pass_recv.at[stage])

    def project(half, side, at):
        start = pl.multiple_of(half * width + side * (width // 2), width // 2)
        return jnp.dot(
            features[half, :, part(side)],
            rows_all[pl.ds(start, width // 2), at],
            preferred_element_type=jnp.float32,
        )

    def tiles(body):
        @pl.loop(0, width // tile)
        def _(i):
            body(pl.ds(pl.multiple_of(i * tile, tile), tile))

    own_gate.wait()
    gate(near, 0)
    weight_end()
    passed(near, 0)

    def first(at):
        totals[:, at] = project(m, near, at) + project(1 - m, near, at)

    tiles(first)
    gate(far, 1)

    def second(at):
        totals[:, at] += project(m, far, at)

    tiles(second)
    passed(far, 1)

    def third(at):
        out[:, at] = (totals[:, at] + project(1 - m, far, at)).astype(out.dtype)

    tiles(third)

    weight_sent()

    most = pl.ds(0, count - 1)
    for slot in (0, 1, 8):
        take(in_signal.at[most], send_sem.at[slot])
    for which in range(2):
        take(in_spec_one.at[0], send_sem.at[5 + which])
    take(arrived, send_sem.at[9])

    @pl.when(g == m)
    def _():
        for which in range(2):
            take(in_spec_one.at[:, most], send_sem.at[2 + which])
            take(in_spec_one.at[0, 0], send_sem.at[2 + which])

    @pl.when(g != m)
    def _():
        for slot in (0, 1, 2):
            take(in_signal.at[0], own_sem.at[slot])
        take(in_skip.at[0], own_sem.at[5])
        take(in_skip.at[1], own_sem.at[3])


def direct_shards(
    signal,
    gate_first,
    gate_second,
    spectrum_first,
    spectrum_second,
    skip_first,
    skip_second,
    out_weight,
):
    count = lax.axis_size("seq")
    span, width = signal.shape
    cols = width // count
    coarse = 2 * count
    strips = 2
    anywhere = pl.BlockSpec(memory_space=pltpu.HBM)
    vmem = pl.BlockSpec(memory_space=pltpu.VMEM)
    bf16, f32 = jnp.bfloat16, jnp.float32
    return pl.pallas_call(
        functools.partial(block_kernel, count),
        out_shape=jax.ShapeDtypeStruct((span, width), bf16),
        in_specs=[anywhere] * 8 + [vmem],
        out_specs=vmem,
        scratch_shapes=[
            pltpu.VMEM((count, span, cols), bf16),
            pltpu.VMEM((count, span, cols), bf16),
            pltpu.VMEM((span, width), bf16),
            pltpu.VMEM((2, count, 2, span, cols), bf16),
            pltpu.VMEM((2, count, 2, span, cols), bf16),
            pltpu.VMEM((2, count, cols), f32),
            pltpu.VMEM((coarse, 2, 2 * span, 2 * span), bf16),
            pltpu.VMEM((coarse, 2, 2 * span, 2 * span), bf16),
            pltpu.VMEM((4, span, span), f32),
            pltpu.VMEM((count + 1, 2 * span, 2 * cols), bf16),
            pltpu.VMEM((coarse, 2 * span, cols), f32),
            pltpu.VMEM((count, span, cols), bf16),
            pltpu.VMEM((count, span, cols), bf16),
            pltpu.VMEM((span, width), bf16),
            pltpu.VMEM((2, span, width), bf16),
            pltpu.VMEM((span, width), f32),
            pltpu.VMEM((2 * width, width), bf16),
            pltpu.SemaphoreType.DMA((10,)),
            pltpu.SemaphoreType.DMA((6,)),
            pltpu.SemaphoreType.DMA((6,)),
            pltpu.SemaphoreType.DMA((2, count)),
            pltpu.SemaphoreType.DMA((2, count)),
            pltpu.SemaphoreType.DMA((2, count)),
            pltpu.SemaphoreType.DMA((2, count)),
            pltpu.SemaphoreType.DMA((1,)),
            pltpu.SemaphoreType.REGULAR((count // 2 - 1,)),
            pltpu.SemaphoreType.DMA((strips,)),
            pltpu.SemaphoreType.DMA((strips,)),
        ],
        compiler_params=pltpu.CompilerParams(
            collective_id=0, has_side_effects=True, vmem_limit_bytes=62 * 1024 * 1024
        ),
        cost_estimate=pl.CostEstimate(
            flops=16 * coarse * span * span * cols, bytes_accessed=1 << 26, transcendentals=0
        ),
    )(
        signal,
        gate_first,
        gate_second,
        spectrum_first,
        spectrum_second,
        skip_first.reshape(count, cols),
        skip_second.reshape(count, cols),
        out_weight,
        jnp.asarray(turn_tables(span, coarse)),
    )


def shards(*arrays):
    count = lax.axis_size("seq")
    span, width = arrays[0].shape
    pairs = lax.axis_size("grp") == 2 and lax.axis_size("mdl") == 2
    whole_tiles = width == count * LANES and span == LANES and count == 8
    if pairs and whole_tiles and arrays[3].shape[1] == 2:
        return direct_shards(*arrays)
    return plain_shards(*arrays)


def solution(mesh):
    placed = (
        P(("grp", "seq"), "mdl"),
        P(("grp", "seq"), "mdl"),
        P(("grp", "seq"), "mdl"),
        P(None, "seq", None, "mdl"),
        P(None, "seq", None, "mdl"),
        P("mdl"),
        P("mdl"),
        P("seq", "mdl"),
    )
    return jax.shard_map(
        shards, mesh=mesh, in_specs=placed, out_specs=P(("grp", "seq"), "mdl"), check_vma=False
    )
```

```python
import functools
import math

import jax
import jax.numpy as jnp
import numpy as np
from jax import lax
from jax.experimental import pallas as pl
from jax.experimental.pallas import tpu as pltpu
from jax.sharding import PartitionSpec as P

MESH = pl.DeviceIdType.MESH
LANES = 128


def angle_grid(first, second, modulus):
    product = first[:, None] * second[None, :] % modulus
    angles = product.astype(jnp.float32) * (2.0 * math.pi / modulus)
    return (jnp.cos(angles), jnp.sin(angles))


def mixing(form, left, right):
    return jnp.einsum(form, left, right, precision=lax.Precision.HIGHEST)


def complex_mix(form, real_table, imag_table, values_re, values_im):
    first_term = mixing(form, real_table, values_re + values_im)
    second_term = mixing(form, real_table + imag_table, values_im)
    third_term = mixing(form, imag_table - real_table, values_re)
    return (first_term - second_term, first_term + third_term)


def channel_filter(field, spectrum):
    coarse = spectrum.shape[1]
    span = spectrum.shape[2]
    count = coarse // 2
    cols = field.shape[1]
    length = coarse * span
    pencil = field.reshape(count, span, cols)
    coarse_ids = jnp.arange(coarse, dtype=jnp.int32)
    cos_a, sin_a = angle_grid(coarse_ids, jnp.arange(count, dtype=jnp.int32), coarse)
    part_re = mixing("ka,amc->kmc", cos_a, pencil)
    part_im = -mixing("ka,amc->kmc", sin_a, pencil)
    fine_ids = jnp.arange(span, dtype=jnp.int32)
    cos_t, sin_t = angle_grid(coarse_ids, fine_ids, length)
    cos_t = cos_t[:, :, None]
    sin_t = sin_t[:, :, None]
    turned_re = part_re * cos_t + part_im * sin_t
    turned_im = part_im * cos_t - part_re * sin_t
    cos_s, sin_s = angle_grid(fine_ids, fine_ids, span)
    full_re, full_im = complex_mix("qm,kmc->kqc", cos_s, -sin_s, turned_re, turned_im)
    filt_re = spectrum[0].astype(jnp.float32)
    filt_im = spectrum[1].astype(jnp.float32)
    prod_re = filt_re * full_re - filt_im * full_im
    prod_im = filt_re * full_im + filt_im * full_re
    inner_re, inner_im = complex_mix("mq,kqc->kmc", cos_s, sin_s, prod_re, prod_im)
    back_re = inner_re * cos_t - inner_im * sin_t
    back_im = inner_im * cos_t + inner_re * sin_t
    result = mixing("ka,kmc->amc", cos_a, back_re) - mixing("ka,kmc->amc", sin_a, back_im)
    return (result / length).reshape(count * span, cols)


def plain_shards(
    signal,
    gate_first,
    gate_second,
    spectrum_first,
    spectrum_second,
    skip_first,
    skip_second,
    out_weight,
):
    seq_index = lax.axis_index("seq")
    width = signal.shape[1]
    parts_seq = lax.axis_size("seq")
    cols = width // parts_seq
    col_sig, col_first, col_second = (
        lax.all_to_all(signal, "seq", split_axis=1, concat_axis=0, tiled=True),
        lax.all_to_all(gate_first, "seq", split_axis=1, concat_axis=0, tiled=True),
        lax.all_to_all(gate_second, "seq", split_axis=1, concat_axis=0, tiled=True),
    )
    spec_one, spec_two = (
        lax.all_to_all(spectrum_first, "seq", split_axis=3, concat_axis=1, tiled=True),
        lax.all_to_all(spectrum_second, "seq", split_axis=3, concat_axis=1, tiled=True),
    )
    skip_one = lax.dynamic_slice_in_dim(skip_first, seq_index * cols, cols, 0)
    skip_two = lax.dynamic_slice_in_dim(skip_second, seq_index * cols, cols, 0)
    values = col_sig.astype(jnp.float32)
    first_conv = channel_filter(values, spec_one) + skip_one * values
    first_out = (col_first.astype(jnp.float32) * first_conv).astype(jnp.bfloat16)
    first_vals = first_out.astype(jnp.float32)
    second_conv = channel_filter(first_vals, spec_two) + skip_two * first_vals
    mixed_cols = (col_second.astype(jnp.float32) * second_conv).astype(jnp.bfloat16)
    mixed = lax.all_to_all(mixed_cols, "seq", split_axis=0, concat_axis=1, tiled=True)
    features = lax.all_gather(mixed, "mdl", axis=1, tiled=True)
    total = jnp.dot(
        features,
        lax.all_gather(out_weight, "seq", axis=0, tiled=True),
        preferred_element_type=jnp.float32,
    )
    return total.astype(jnp.bfloat16)


def turn_tables(span, coarse):
    ids = np.arange(span)
    fine = 2.0 * math.pi * (ids[:, None] * ids[None, :] % span) / span
    step = 2.0 * math.pi * np.broadcast_to(ids[:, None], (span, span)) / (span * coarse)
    return np.stack(
        [np.cos(fine), np.sin(fine), np.cos(step), np.sin(step), np.cos(step).T, np.sin(step).T]
    ).astype(np.float32)


def weighted(terms):
    total = None
    for weight, value in terms:
        if abs(weight) < 1e-12:
            continue
        if abs(weight - 1.0) < 1e-12:
            term = value
        elif abs(weight + 1.0) < 1e-12:
            total = -value if total is None else total - value
            continue
        else:
            term = value * weight
        total = term if total is None else total + term
    return total


def coarse_forward(field, parts, rows):
    count, span, cols = field.shape
    half = count // 2

    @pl.loop(0, span // rows)
    def _(i):
        at = pl.multiple_of(i * rows, rows)
        f = [field[a, pl.ds(at, rows), :].astype(jnp.float32) for a in range(count)]
        plus = {a: f[a] + f[count - a] for a in range(1, half)}
        minus = {a: f[a] - f[count - a] for a in range(1, half)}
        for j in range(count + 1):
            for_cos, for_sin = (plus, minus) if j % 2 == 0 else (minus, plus)
            angle = [math.pi * a * j / count for a in range(count)]
            real = weighted(
                [(1.0, f[0]), (math.cos(angle[half]), f[half])]
                + [(math.cos(angle[a]), for_cos[a]) for a in range(1, half)]
            )
            imag = weighted(
                [(-math.sin(angle[half]), f[half])]
                + [(-math.sin(angle[a]), for_sin[a]) for a in range(1, half)]
            )
            if imag is None:
                imag = jnp.zeros_like(real)
            for top, value in ((at, real), (pl.multiple_of(span + at, rows), imag)):
                high = value.astype(jnp.bfloat16)
                parts[j, pl.ds(top, rows), :cols] = high
                parts[j, pl.ds(top, rows), cols:] = (value - high.astype(jnp.float32)).astype(
                    jnp.bfloat16
                )


def split_dot(table, j, both, cols):
    main = jnp.dot(table[j, 0], both, preferred_element_type=jnp.float32)
    rest = jnp.dot(table[j, 1], both[:, :cols], preferred_element_type=jnp.float32)
    return main[:, :cols] + (main[:, cols:] + rest)


def fine_stage(parts, spectrum, there, back_table, back, own, arrive, pass_over, passed):
    half = back.shape[0] // 2
    span, cols = spectrum.shape[3], spectrum.shape[4]

    def one(k, b):
        j = 2 * b + k
        source = jnp.where(j <= half, j, 2 * half - j)
        full = split_dot(there, j, parts[source], cols)
        full_re, full_im = full[:span], full[span:]
        filt_re = spectrum[k, b, 0].astype(jnp.float32)
        filt_im = spectrum[k, b, 1].astype(jnp.float32)
        prod_re = filt_re * full_re - filt_im * full_im
        prod_im = filt_re * full_im + filt_im * full_re
        prod = jnp.concatenate([prod_re, prod_im], axis=0)
        high = prod.astype(jnp.bfloat16)
        low = (prod - high.astype(jnp.float32)).astype(jnp.bfloat16)
        both = jnp.concatenate([high, low], axis=1)
        back[j] = split_dot(back_table, j, both, cols)

    @pl.loop(0, half // 2)
    def _(v):
        blocks = arrive(v)
        for b in blocks:
            pass_over(b)
        for b in blocks:
            one(own, b)
        for b in blocks:
            passed(b)
        for b in blocks:
            one(1 - own, b)


def coarse_back(back, field, gate, skip, result, rows, wanted=None):
    count, span, cols = field.shape
    half = count // 2
    direct = jnp.broadcast_to(skip, (rows, cols))

    @pl.loop(0, span // rows)
    def _(i):
        at = pl.multiple_of(i * rows, rows)
        low = pl.multiple_of(span + at, rows)

        def real(j):
            return back[j, pl.ds(at, rows), :]

        def imag(j):
            return back[j, pl.ds(low, rows), :]

        re = [real(0)] + [real(j) + real(2 * count - j) for j in range(1, count)] + [real(count)]
        im = [None] + [imag(j) - imag(2 * count - j) for j in range(1, count)] + [None]
        even_re = [re[j] + re[count - j] for j in range(half)]
        odd_re = [re[j] - re[count - j] for j in range(half)]
        even_im = [None] + [im[j] - im[count - j] for j in range(1, half)]
        odd_im = [None] + [im[j] + im[count - j] for j in range(1, half)]
        for a in range(count) if wanted is None else wanted:
            use_re, use_im = (even_re, even_im) if a % 2 == 0 else (odd_re, odd_im)
            angle = [math.pi * a * j / count for j in range(half + 1)]
            total = weighted(
                [(math.cos(angle[j]), use_re[j]) for j in range(half)]
                + [(math.cos(angle[half]), re[half]), (-math.sin(angle[half]), im[half])]
                + [(-math.sin(angle[j]), use_im[j]) for j in range(1, half)]
            )
            values = field[a, pl.ds(at, rows), :].astype(jnp.float32)
            total = total + direct * values
            if gate is not None:
                total = gate[a, pl.ds(at, rows), :].astype(jnp.float32) * total
            result[a, pl.ds(at, rows), :] = total.astype(jnp.bfloat16)


def build_tables(tab, there, back_table, turn, count, span):
    turn[0] = tab[0]
    turn[1] = tab[1]
    turn[2] = tab[0]
    turn[3] = tab[1]
    scale = 1.0 / (2 * count * span)

    @pl.loop(0, 2 * count)
    def _(j):
        flip = jnp.where(j > count, -1.0, 1.0).astype(jnp.float32)
        cos_a, sin_a, cos_b, sin_b = turn[0], turn[1], turn[2], turn[3]
        cos_s, sin_s = cos_b * scale, sin_b * scale
        entries = (
            (there, cos_a, sin_a * flip, -sin_a, cos_a * flip),
            (back_table, cos_s, -sin_s, sin_s, cos_s),
        )
        places = ((0, 0), (0, 1), (1, 0), (1, 1))
        for table, *blocks in entries:
            for (row, col), value in zip(places, blocks):
                at = (slice(row * span, row * span + span), slice(col * span, col * span + span))
                high = value.astype(jnp.bfloat16)
                table[(j, 0) + at] = high
                table[(j, 1) + at] = (value - high.astype(jnp.float32)).astype(jnp.bfloat16)
        turn[0] = cos_a * tab[4] - sin_a * tab[5]
        turn[1] = sin_a * tab[4] + cos_a * tab[5]
        turn[2] = cos_b * tab[2] - sin_b * tab[3]
        turn[3] = sin_b * tab[2] + cos_b * tab[3]


def block_kernel(
    count,
    signal,
    gate_one,
    gate_two,
    spec_one,
    spec_two,
    skip_one,
    skip_two,
    weight,
    tab,
    out,
    in_signal,
    in_gate_one,
    in_gate_two,
    in_spec_one,
    in_spec_two,
    in_skip,
    there,
    back_table,
    turn,
    parts,
    back,
    second_field,
    mixed,
    arrived,
    features,
    totals,
    rows_all,
    send_sem,
    own_sem,
    recv_sem,
    spec_recv,
    relay_recv,
    weight_recv,
    plane_recv,
    whole_recv,
    known_sem,
    mix_recv,
    pass_recv,
):
    g, s, m = lax.axis_index("grp"), lax.axis_index("seq"), lax.axis_index("mdl")
    span, cols = in_signal.shape[1], in_signal.shape[2]
    levels = count // 2
    z, x = s // 2, lax.rem(s, 2)
    above, below = z < levels - 1, z > 0
    beside_levels = jnp.where(above & below, 2, 1)

    def tell_levels(sem):
        @pl.when(above)
        def _():
            pl.semaphore_signal(sem, inc=1, device_id=(g, s + 2, m), device_id_type=MESH)

        @pl.when(below)
        def _():
            pl.semaphore_signal(sem, inc=1, device_id=(g, s - 2, m), device_id_type=MESH)

    barrier = pltpu.get_barrier_semaphore()
    tell_levels(barrier)

    @pl.loop(1, 8)
    def _(o):
        peer = lax.rem((g * 2 + x) * 2 + m + o, 8)
        pl.semaphore_signal(
            barrier,
            inc=1,
            device_id=(peer // 4, 2 * z + lax.rem(peer // 2, 2), lax.rem(peer, 2)),
            device_id_type=MESH,
        )

    pl.semaphore_wait(barrier, 7 + beside_levels)

    def hear_levels(r):
        tell_levels(known_sem.at[r])
        pl.semaphore_wait(known_sem.at[r], beside_levels)

    def level(v):
        return 2 * lax.rem(z // 2 + v // 2, 2) + lax.rem(z + v, 2)

    def columns(block):
        return pl.ds(pl.multiple_of(block * cols, cols), cols)

    def remote(source, target, send, recv, where):
        return pltpu.make_async_remote_copy(
            src_ref=source,
            dst_ref=target,
            send_sem=send,
            recv_sem=recv,
            device_id=where,
            device_id_type=MESH,
        )

    def local(source, target, recv):
        return pltpu.make_async_copy(source, target, recv)

    def take(view, sem):
        pltpu.make_async_copy(view, view, sem).wait()

    def swap(source, target, slot):
        @pl.when(g == m)
        def _():
            local(source, target, recv_sem.at[slot]).start()

        @pl.when(g != m)
        def _():
            remote(source, target, own_sem.at[slot], recv_sem.at[slot], (m, s, g)).start()

    def others(levels_apart=(2, 3, 1, 0)):
        for v in levels_apart:
            for side in (1 - x, x)[: 2 if v else 1]:
                yield 2 * level(v) + side

    def send_rows(array, buffer, slot, levels_apart=(2, 3, 1, 0)):
        for c in others(levels_apart):
            remote(
                array.at[:, columns(c)],
                buffer.at[s],
                send_sem.at[slot],
                recv_sem.at[slot],
                (m, c, g),
            ).start()
        if 0 in levels_apart:
            swap(array.at[:, columns(s)], buffer.at[s], slot)

    def send_spectrum(array, buffer, slot, which):
        recv = spec_recv.at[which, s]

        @pl.when(g == m)
        def _():
            for c in others():
                for k in range(2):
                    remote(
                        array.at[:, k, :, columns(c)],
                        buffer.at[k, s],
                        send_sem.at[slot],
                        recv,
                        (g, c, k),
                    ).start()
            source = array.at[:, 1 - m, :, columns(s)]
            remote(source, buffer.at[1 - m, s], send_sem.at[slot], recv, (g, s, 1 - m)).start()
            local(array.at[:, m, :, columns(s)], buffer.at[m, s], recv).start()

    beside = s + 1 - 2 * x
    depth = weight.shape[0]
    pieces = weight_recv.shape[0]
    piece = depth // 2 // pieces

    def chunk(block, p, half=None):
        at = block * depth + (g if half is None else half) * (depth // 2) + p * piece
        return rows_all.at[pl.ds(pl.multiple_of(at, piece), piece), :]

    def whole(block):
        return rows_all.at[pl.ds(pl.multiple_of(block * depth, depth), depth), :]

    def on_line(v):
        return 2 * level(v) + x

    def post(block, p, source, where, slot):
        remote(
            source, chunk(block, p), send_sem.at[7], weight_recv.at[p, slot], (g, where, m)
        ).start()

    def over(block, p):
        view = chunk(block, p)
        remote(view, view, own_sem.at[4], plane_recv.at[p, block], (1 - g, s, m)).start()

    def landed(block, p, slot):
        take(chunk(block, p), weight_recv.at[p, slot])

    def own_piece(p):
        at = g * (depth // 2) + p * piece
        return weight.at[pl.ds(pl.multiple_of(at, piece), piece), :]

    def weight_cross(inner):
        @pl.when((above & below) if inner else jnp.logical_not(above & below))
        def _():
            for p in range(pieces):
                post(s, p, own_piece(p), on_line(3), 3)

    def weight_own():
        for p in range(pieces):
            post(s, p, own_piece(p), on_line(1), 1)
        local(weight, whole(s), whole_recv.at[0]).start()

    def weight_beside():
        for p in range(pieces):
            post(s, p, own_piece(p), beside, 4)

    def weight_near(p):
        block = on_line(1)
        landed(block, p, 1)
        post(block, p, chunk(block, p), beside, 5)
        over(block, p)

    def weight_far(p):
        block = on_line(3)
        landed(block, p, 3)
        post(block, p, chunk(block, p), on_line(1), 2)
        post(block, p, chunk(block, p), beside, 7)
        over(block, p)

    def weight_last(p):
        block = on_line(2)
        landed(block, p, 2)
        post(block, p, chunk(block, p), beside, 6)
        over(block, p)

    def weight_side(p, v):
        block = 2 * level(v) + 1 - x
        landed(block, p, 4 + v)
        over(block, p)

    def weight_end():
        take(whole(s), whole_recv.at[0])
        for p in range(pieces):
            for v in range(levels):
                for side in (x, 1 - x)[v == 0 :]:
                    block = 2 * level(v) + side
                    take(chunk(block, p, 1 - g), plane_recv.at[p, block])

    def weight_sent():
        rows = rows_all.at[pl.ds(0, 7 * (depth // 2)), :]
        take(rows, send_sem.at[7])
        take(rows, own_sem.at[4])

    def relay(buffer, which, b):
        return remote(
            buffer.at[m, b],
            buffer.at[m, b],
            send_sem.at[5 + which],
            relay_recv.at[which, b],
            (g, s, 1 - m),
        )

    def fine(buffer, which):
        def arrive(v):
            blocks = (2 * level(v) + x, 2 * level(v) + 1 - x)
            for b in blocks:
                take(buffer.at[m, b], spec_recv.at[which, b])
            return blocks

        def pass_over(b):
            relay(buffer, which, b).start()

        def passed(b):
            take(buffer.at[1 - m, b], relay_recv.at[which, b])

        fine_stage(parts, buffer, there, back_table, back, m, arrive, pass_over, passed)

    own_gate = local(gate_two, in_gate_two, recv_sem.at[4])
    own_gate = local(gate_two, in_gate_two, recv_sem.at[4])
    weight_cross(True)
    weight_own()
    weight_beside()
    hear_levels(0)

    @pl.when(above & below)
    def _():
        send_rows(signal, in_signal, 0, (3,))

    send_rows(signal, in_signal, 0, (1, 0))
    hear_levels(1)
    send_rows(signal, in_signal, 0, (2,))
    hear_levels(2)
    weight_cross(False)

    @pl.when(jnp.logical_not(above & below))
    def _():
        send_rows(signal, in_signal, 0, (3,))

    send_spectrum(spec_one, in_spec_one, 2, 0)
    build_tables(tab, there, back_table, turn, count, span)
    weight_near(0)
    weight_near(1)
    weight_side(0, 0)
    weight_side(1, 0)
    weight_far(0)
    weight_far(1)
    send_rows(gate_one, in_gate_one, 1)
    send_spectrum(spec_two, in_spec_two, 3, 1)
    weight_last(0)
    weight_last(1)
    own_gate.start()
    swap(skip_one, in_skip.at[0], 5)
    swap(skip_two, in_skip.at[1], 3)
    take(in_signal, recv_sem.at[0])
    coarse_forward(in_signal, parts, 16)
    weight_side(0, 1)
    weight_side(1, 1)
    fine(in_spec_one, 0)
    weight_side(0, 3)
    weight_side(1, 3)
    take(in_gate_one, recv_sem.at[1])
    take(in_skip.at[0], recv_sem.at[5])
    take(in_skip.at[1], recv_sem.at[3])
    mine = pl.ds(s, 1)
    coarse_back(back, in_signal, in_gate_one, in_skip[0, mine, :], second_field, 16)
    coarse_forward(second_field, parts, 16)
    weight_side(0, 2)
    weight_side(1, 2)
    fine(in_spec_two, 1)

    skip = in_skip[1, mine, :]

    width = count * cols
    tile = 2 * cols
    near, far = z // 2, 1 - z // 2

    def deliver(c, stage, own):
        return remote(
            mixed.at[c],
            arrived.at[:, columns(s)],
            own_sem.at[2] if own else send_sem.at[8],
            mix_recv.at[stage],
            (m, c, g),
        )

    def finish(low):
        wanted = range(count // 2) if low else range(count // 2, count)
        coarse_back(back, second_field, None, skip, mixed, 16, wanted)

    for stage in (1, 0):
        for low in (False, True):

            @pl.when((z < levels // 2) if low == (stage == 0) else (z >= levels // 2))
            def _():
                finish(low)

        for c in others((2, 3) if stage else (1, 0)):
            deliver(c, stage, False).start()

    @pl.when(g == m)
    def _():
        local(mixed.at[s], arrived.at[:, columns(s)], mix_recv.at[0]).start()

    @pl.when(g != m)
    def _():
        deliver(s, 0, True).start()

    def part(side):
        return pl.ds(pl.multiple_of(side * (width // 2), width // 2), width // 2)

    def gate(side, stage):
        at = part(side)
        take(arrived.at[:, at], mix_recv.at[stage])
        gated = in_gate_two[:, at].astype(jnp.float32) * arrived[:, at].astype(jnp.float32)
        features[m, :, at] = gated.astype(jnp.bfloat16)
        view = features.at[m, :, at]
        remote(view, view, send_sem.at[9], pass_recv.at[stage], (g, s, 1 - m)).start()

    def passed(side, stage):
        take(features.at[1 - m, :, part(side)], pass_recv.at[stage])

    def project(half, side, at):
        start = pl.multiple_of(half * width + side * (width // 2), width // 2)
        return jnp.dot(
            features[half, :, part(side)],
            rows_all[pl.ds(start, width // 2), at],
            preferred_element_type=jnp.float32,
        )

    def tiles(body):
        @pl.loop(0, width // tile)
        def _(i):
            body(pl.ds(pl.multiple_of(i * tile, tile), tile))

    own_gate.wait()
    gate(near, 0)
    weight_end()
    passed(near, 0)

    def first(at):
        totals[:, at] = project(m, near, at) + project(1 - m, near, at)

    tiles(first)
    gate(far, 1)

    def second(at):
        totals[:, at] += project(m, far, at)

    tiles(second)
    passed(far, 1)

    def third(at):
        out[:, at] = (totals[:, at] + project(1 - m, far, at)).astype(out.dtype)

    tiles(third)

    weight_sent()

    most = pl.ds(0, count - 1)
    for slot in (0, 1, 8):
        take(in_signal.at[most], send_sem.at[slot])
    for which in range(2):
        take(in_spec_one.at[0], send_sem.at[5 + which])
    take(arrived, send_sem.at[9])

    @pl.when(g == m)
    def _():
        for which in range(2):
            take(in_spec_one.at[:, most], send_sem.at[2 + which])
            take(in_spec_one.at[0, 0], send_sem.at[2 + which])

    @pl.when(g != m)
    def _():
        for slot in (0, 1, 2):
            take(in_signal.at[0], own_sem.at[slot])
        take(in_skip.at[0], own_sem.at[5])
        take(in_skip.at[1], own_sem.at[3])


def direct_shards(
    signal,
    gate_first,
    gate_second,
    spectrum_first,
    spectrum_second,
    skip_first,
    skip_second,
    out_weight,
):
    count = lax.axis_size("seq")
    span, width = signal.shape
    cols = width // count
    coarse = 2 * count
    strips = 2
    anywhere = pl.BlockSpec(memory_space=pltpu.HBM)
    vmem = pl.BlockSpec(memory_space=pltpu.VMEM)
    bf16, f32 = jnp.bfloat16, jnp.float32
    return pl.pallas_call(
        functools.partial(block_kernel, count),
        out_shape=jax.ShapeDtypeStruct((span, width), bf16),
        in_specs=[anywhere] * 8 + [vmem],
        out_specs=vmem,
        scratch_shapes=[
            pltpu.VMEM((count, span, cols), bf16),
            pltpu.VMEM((count, span, cols), bf16),
            pltpu.VMEM((span, width), bf16),
            pltpu.VMEM((2, count, 2, span, cols), bf16),
            pltpu.VMEM((2, count, 2, span, cols), bf16),
            pltpu.VMEM((2, count, cols), f32),
            pltpu.VMEM((coarse, 2, 2 * span, 2 * span), bf16),
            pltpu.VMEM((coarse, 2, 2 * span, 2 * span), bf16),
            pltpu.VMEM((4, span, span), f32),
            pltpu.VMEM((count + 1, 2 * span, 2 * cols), bf16),
            pltpu.VMEM((coarse, 2 * span, cols), f32),
            pltpu.VMEM((count, span, cols), bf16),
            pltpu.VMEM((count, span, cols), bf16),
            pltpu.VMEM((span, width), bf16),
            pltpu.VMEM((2, span, width), bf16),
            pltpu.VMEM((span, width), f32),
            pltpu.VMEM((2 * width, width), bf16),
            pltpu.SemaphoreType.DMA((10,)),
            pltpu.SemaphoreType.DMA((6,)),
            pltpu.SemaphoreType.DMA((6,)),
            pltpu.SemaphoreType.DMA((2, count)),
            pltpu.SemaphoreType.DMA((2, count)),
            pltpu.SemaphoreType.DMA((2, count)),
            pltpu.SemaphoreType.DMA((2, count)),
            pltpu.SemaphoreType.DMA((1,)),
            pltpu.SemaphoreType.REGULAR((count // 2 - 1,)),
            pltpu.SemaphoreType.DMA((strips,)),
            pltpu.SemaphoreType.DMA((strips,)),
        ],
        compiler_params=pltpu.CompilerParams(
            collective_id=0, has_side_effects=True, vmem_limit_bytes=62 * 1024 * 1024
        ),
        cost_estimate=pl.CostEstimate(
            flops=16 * coarse * span * span * cols, bytes_accessed=1 << 26, transcendentals=0
        ),
    )(
        signal,
        gate_first,
        gate_second,
        spectrum_first,
        spectrum_second,
        skip_first.reshape(count, cols),
        skip_second.reshape(count, cols),
        out_weight,
        jnp.asarray(turn_tables(span, coarse)),
    )


def shards(*arrays):
    count = lax.axis_size("seq")
    span, width = arrays[0].shape
    pairs = lax.axis_size("grp") == 2 and lax.axis_size("mdl") == 2
    whole_tiles = width == count * LANES and span == LANES and count == 8
    if pairs and whole_tiles and arrays[3].shape[1] == 2:
        return direct_shards(*arrays)
    return plain_shards(*arrays)


def solution(mesh):
    placed = (
        P(("grp", "seq"), "mdl"),
        P(("grp", "seq"), "mdl"),
        P(("grp", "seq"), "mdl"),
        P(None, "seq", None, "mdl"),
        P(None, "seq", None, "mdl"),
        P("mdl"),
        P("mdl"),
        P("seq", "mdl"),
    )
    return jax.shard_map(
        shards, mesh=mesh, in_specs=placed, out_specs=P(("grp", "seq"), "mdl"), check_vma=False
    )
```

```python
import functools
import math

import jax
import jax.numpy as jnp
import numpy as np
from jax import lax
from jax.experimental import pallas as pl
from jax.experimental.pallas import tpu as pltpu
from jax.sharding import PartitionSpec as P

MESH = pl.DeviceIdType.MESH
LANES = 128


def angle_grid(first, second, modulus):
    product = first[:, None] * second[None, :] % modulus
    angles = product.astype(jnp.float32) * (2.0 * math.pi / modulus)
    return (jnp.cos(angles), jnp.sin(angles))


def mixing(form, left, right):
    return jnp.einsum(form, left, right, precision=lax.Precision.HIGHEST)


def complex_mix(form, real_table, imag_table, values_re, values_im):
    first_term = mixing(form, real_table, values_re + values_im)
    second_term = mixing(form, real_table + imag_table, values_im)
    third_term = mixing(form, imag_table - real_table, values_re)
    return (first_term - second_term, first_term + third_term)


def channel_filter(field, spectrum):
    coarse = spectrum.shape[1]
    span = spectrum.shape[2]
    count = coarse // 2
    cols = field.shape[1]
    length = coarse * span
    pencil = field.reshape(count, span, cols)
    coarse_ids = jnp.arange(coarse, dtype=jnp.int32)
    cos_a, sin_a = angle_grid(coarse_ids, jnp.arange(count, dtype=jnp.int32), coarse)
    part_re = mixing("ka,amc->kmc", cos_a, pencil)
    part_im = -mixing("ka,amc->kmc", sin_a, pencil)
    fine_ids = jnp.arange(span, dtype=jnp.int32)
    cos_t, sin_t = angle_grid(coarse_ids, fine_ids, length)
    cos_t = cos_t[:, :, None]
    sin_t = sin_t[:, :, None]
    turned_re = part_re * cos_t + part_im * sin_t
    turned_im = part_im * cos_t - part_re * sin_t
    cos_s, sin_s = angle_grid(fine_ids, fine_ids, span)
    full_re, full_im = complex_mix("qm,kmc->kqc", cos_s, -sin_s, turned_re, turned_im)
    filt_re = spectrum[0].astype(jnp.float32)
    filt_im = spectrum[1].astype(jnp.float32)
    prod_re = filt_re * full_re - filt_im * full_im
    prod_im = filt_re * full_im + filt_im * full_re
    inner_re, inner_im = complex_mix("mq,kqc->kmc", cos_s, sin_s, prod_re, prod_im)
    back_re = inner_re * cos_t - inner_im * sin_t
    back_im = inner_im * cos_t + inner_re * sin_t
    result = mixing("ka,kmc->amc", cos_a, back_re) - mixing("ka,kmc->amc", sin_a, back_im)
    return (result / length).reshape(count * span, cols)


def plain_shards(
    signal,
    gate_first,
    gate_second,
    spectrum_first,
    spectrum_second,
    skip_first,
    skip_second,
    out_weight,
):
    seq_index = lax.axis_index("seq")
    width = signal.shape[1]
    parts_seq = lax.axis_size("seq")
    cols = width // parts_seq
    col_sig, col_first, col_second = (
        lax.all_to_all(signal, "seq", split_axis=1, concat_axis=0, tiled=True),
        lax.all_to_all(gate_first, "seq", split_axis=1, concat_axis=0, tiled=True),
        lax.all_to_all(gate_second, "seq", split_axis=1, concat_axis=0, tiled=True),
    )
    spec_one, spec_two = (
        lax.all_to_all(spectrum_first, "seq", split_axis=3, concat_axis=1, tiled=True),
        lax.all_to_all(spectrum_second, "seq", split_axis=3, concat_axis=1, tiled=True),
    )
    skip_one = lax.dynamic_slice_in_dim(skip_first, seq_index * cols, cols, 0)
    skip_two = lax.dynamic_slice_in_dim(skip_second, seq_index * cols, cols, 0)
    values = col_sig.astype(jnp.float32)
    first_conv = channel_filter(values, spec_one) + skip_one * values
    first_out = (col_first.astype(jnp.float32) * first_conv).astype(jnp.bfloat16)
    first_vals = first_out.astype(jnp.float32)
    second_conv = channel_filter(first_vals, spec_two) + skip_two * first_vals
    mixed_cols = (col_second.astype(jnp.float32) * second_conv).astype(jnp.bfloat16)
    mixed = lax.all_to_all(mixed_cols, "seq", split_axis=0, concat_axis=1, tiled=True)
    features = lax.all_gather(mixed, "mdl", axis=1, tiled=True)
    total = jnp.dot(
        features,
        lax.all_gather(out_weight, "seq", axis=0, tiled=True),
        preferred_element_type=jnp.float32,
    )
    return total.astype(jnp.bfloat16)


def turn_tables(span, coarse):
    ids = np.arange(span)
    fine = 2.0 * math.pi * (ids[:, None] * ids[None, :] % span) / span
    step = 2.0 * math.pi * np.broadcast_to(ids[:, None], (span, span)) / (span * coarse)
    return np.stack(
        [np.cos(fine), np.sin(fine), np.cos(step), np.sin(step), np.cos(step).T, np.sin(step).T]
    ).astype(np.float32)


def weighted(terms):
    total = None
    for weight, value in terms:
        if abs(weight) < 1e-12:
            continue
        if abs(weight - 1.0) < 1e-12:
            term = value
        elif abs(weight + 1.0) < 1e-12:
            total = -value if total is None else total - value
            continue
        else:
            term = value * weight
        total = term if total is None else total + term
    return total


def coarse_forward(field, parts, rows):
    count, span, cols = field.shape
    half = count // 2

    @pl.loop(0, span // rows)
    def _(i):
        at = pl.multiple_of(i * rows, rows)
        f = [field[a, pl.ds(at, rows), :].astype(jnp.float32) for a in range(count)]
        plus = {a: f[a] + f[count - a] for a in range(1, half)}
        minus = {a: f[a] - f[count - a] for a in range(1, half)}
        for j in range(count + 1):
            for_cos, for_sin = (plus, minus) if j % 2 == 0 else (minus, plus)
            angle = [math.pi * a * j / count for a in range(count)]
            real = weighted(
                [(1.0, f[0]), (math.cos(angle[half]), f[half])]
                + [(math.cos(angle[a]), for_cos[a]) for a in range(1, half)]
            )
            imag = weighted(
                [(-math.sin(angle[half]), f[half])]
                + [(-math.sin(angle[a]), for_sin[a]) for a in range(1, half)]
            )
            if imag is None:
                imag = jnp.zeros_like(real)
            for top, value in ((at, real), (pl.multiple_of(span + at, rows), imag)):
                high = value.astype(jnp.bfloat16)
                parts[j, pl.ds(top, rows), :cols] = high
                parts[j, pl.ds(top, rows), cols:] = (value - high.astype(jnp.float32)).astype(
                    jnp.bfloat16
                )


def split_dot(table, j, both, cols):
    main = jnp.dot(table[j, 0], both, preferred_element_type=jnp.float32)
    rest = jnp.dot(table[j, 1], both[:, :cols], preferred_element_type=jnp.float32)
    return main[:, :cols] + (main[:, cols:] + rest)


def fine_stage(parts, spectrum, there, back_table, back, own, arrive, pass_over, passed):
    half = back.shape[0] // 2
    span, cols = spectrum.shape[3], spectrum.shape[4]

    def one(k, b):
        j = 2 * b + k
        source = jnp.where(j <= half, j, 2 * half - j)
        full = split_dot(there, j, parts[source], cols)
        full_re, full_im = full[:span], full[span:]
        filt_re = spectrum[k, b, 0].astype(jnp.float32)
        filt_im = spectrum[k, b, 1].astype(jnp.float32)
        prod_re = filt_re * full_re - filt_im * full_im
        prod_im = filt_re * full_im + filt_im * full_re
        prod = jnp.concatenate([prod_re, prod_im], axis=0)
        high = prod.astype(jnp.bfloat16)
        low = (prod - high.astype(jnp.float32)).astype(jnp.bfloat16)
        both = jnp.concatenate([high, low], axis=1)
        back[j] = split_dot(back_table, j, both, cols)

    @pl.loop(0, half // 2)
    def _(v):
        blocks = arrive(v)
        for b in blocks:
            pass_over(b)
        for b in blocks:
            one(own, b)
        for b in blocks:
            passed(b)
        for b in blocks:
            one(1 - own, b)


def coarse_back(back, field, gate, skip, result, rows, wanted=None):
    count, span, cols = field.shape
    half = count // 2
    direct = jnp.broadcast_to(skip, (rows, cols))

    @pl.loop(0, span // rows)
    def _(i):
        at = pl.multiple_of(i * rows, rows)
        low = pl.multiple_of(span + at, rows)

        def real(j):
            return back[j, pl.ds(at, rows), :]

        def imag(j):
            return back[j, pl.ds(low, rows), :]

        re = [real(0)] + [real(j) + real(2 * count - j) for j in range(1, count)] + [real(count)]
        im = [None] + [imag(j) - imag(2 * count - j) for j in range(1, count)] + [None]
        even_re = [re[j] + re[count - j] for j in range(half)]
        odd_re = [re[j] - re[count - j] for j in range(half)]
        even_im = [None] + [im[j] - im[count - j] for j in range(1, half)]
        odd_im = [None] + [im[j] + im[count - j] for j in range(1, half)]
        for a in range(count) if wanted is None else wanted:
            use_re, use_im = (even_re, even_im) if a % 2 == 0 else (odd_re, odd_im)
            angle = [math.pi * a * j / count for j in range(half + 1)]
            total = weighted(
                [(math.cos(angle[j]), use_re[j]) for j in range(half)]
                + [(math.cos(angle[half]), re[half]), (-math.sin(angle[half]), im[half])]
                + [(-math.sin(angle[j]), use_im[j]) for j in range(1, half)]
            )
            values = field[a, pl.ds(at, rows), :].astype(jnp.float32)
            total = total + direct * values
            if gate is not None:
                total = gate[a, pl.ds(at, rows), :].astype(jnp.float32) * total
            result[a, pl.ds(at, rows), :] = total.astype(jnp.bfloat16)


def build_tables(tab, there, back_table, turn, count, span):
    turn[0] = tab[0]
    turn[1] = tab[1]
    turn[2] = tab[0]
    turn[3] = tab[1]
    scale = 1.0 / (2 * count * span)

    @pl.loop(0, 2 * count)
    def _(j):
        flip = jnp.where(j > count, -1.0, 1.0).astype(jnp.float32)
        cos_a, sin_a, cos_b, sin_b = turn[0], turn[1], turn[2], turn[3]
        cos_s, sin_s = cos_b * scale, sin_b * scale
        entries = (
            (there, cos_a, sin_a * flip, -sin_a, cos_a * flip),
            (back_table, cos_s, -sin_s, sin_s, cos_s),
        )
        places = ((0, 0), (0, 1), (1, 0), (1, 1))
        for table, *blocks in entries:
            for (row, col), value in zip(places, blocks):
                at = (slice(row * span, row * span + span), slice(col * span, col * span + span))
                high = value.astype(jnp.bfloat16)
                table[(j, 0) + at] = high
                table[(j, 1) + at] = (value - high.astype(jnp.float32)).astype(jnp.bfloat16)
        turn[0] = cos_a * tab[4] - sin_a * tab[5]
        turn[1] = sin_a * tab[4] + cos_a * tab[5]
        turn[2] = cos_b * tab[2] - sin_b * tab[3]
        turn[3] = sin_b * tab[2] + cos_b * tab[3]


def block_kernel(
    count,
    signal,
    gate_one,
    gate_two,
    spec_one,
    spec_two,
    skip_one,
    skip_two,
    weight,
    tab,
    out,
    in_signal,
    in_gate_one,
    in_gate_two,
    in_spec_one,
    in_spec_two,
    in_skip,
    there,
    back_table,
    turn,
    parts,
    back,
    second_field,
    mixed,
    arrived,
    features,
    totals,
    rows_all,
    send_sem,
    own_sem,
    recv_sem,
    spec_recv,
    relay_recv,
    weight_recv,
    plane_recv,
    whole_recv,
    known_sem,
    mix_recv,
    pass_recv,
):
    g, s, m = lax.axis_index("grp"), lax.axis_index("seq"), lax.axis_index("mdl")
    span, cols = in_signal.shape[1], in_signal.shape[2]
    levels = count // 2
    z, x = s // 2, lax.rem(s, 2)
    above, below = z < levels - 1, z > 0
    beside_levels = jnp.where(above & below, 2, 1)

    def tell_levels(sem):
        @pl.when(above)
        def _():
            pl.semaphore_signal(sem, inc=1, device_id=(g, s + 2, m), device_id_type=MESH)

        @pl.when(below)
        def _():
            pl.semaphore_signal(sem, inc=1, device_id=(g, s - 2, m), device_id_type=MESH)

    barrier = pltpu.get_barrier_semaphore()
    tell_levels(barrier)

    @pl.loop(1, 8)
    def _(o):
        peer = lax.rem((g * 2 + x) * 2 + m + o, 8)
        pl.semaphore_signal(
            barrier,
            inc=1,
            device_id=(peer // 4, 2 * z + lax.rem(peer // 2, 2), lax.rem(peer, 2)),
            device_id_type=MESH,
        )

    pl.semaphore_wait(barrier, 7 + beside_levels)

    def hear_levels(r):
        tell_levels(known_sem.at[r])
        pl.semaphore_wait(known_sem.at[r], beside_levels)

    def level(v):
        return 2 * lax.rem(z // 2 + v // 2, 2) + lax.rem(z + v, 2)

    def columns(block):
        return pl.ds(pl.multiple_of(block * cols, cols), cols)

    def remote(source, target, send, recv, where):
        return pltpu.make_async_remote_copy(
            src_ref=source,
            dst_ref=target,
            send_sem=send,
            recv_sem=recv,
            device_id=where,
            device_id_type=MESH,
        )

    def local(source, target, recv):
        return pltpu.make_async_copy(source, target, recv)

    def take(view, sem):
        pltpu.make_async_copy(view, view, sem).wait()

    def swap(source, target, slot):
        @pl.when(g == m)
        def _():
            local(source, target, recv_sem.at[slot]).start()

        @pl.when(g != m)
        def _():
            remote(source, target, own_sem.at[slot], recv_sem.at[slot], (m, s, g)).start()

    def others(levels_apart=(2, 3, 1, 0)):
        for v in levels_apart:
            for side in (1 - x, x)[: 2 if v else 1]:
                yield 2 * level(v) + side

    def send_rows(array, buffer, slot, levels_apart=(2, 3, 1, 0)):
        for c in others(levels_apart):
            remote(
                array.at[:, columns(c)],
                buffer.at[s],
                send_sem.at[slot],
                recv_sem.at[slot],
                (m, c, g),
            ).start()
        if 0 in levels_apart:
            swap(array.at[:, columns(s)], buffer.at[s], slot)

    def send_spectrum(array, buffer, slot, which):
        recv = spec_recv.at[which, s]

        @pl.when(g == m)
        def _():
            for c in others():
                for k in range(2):
                    remote(
                        array.at[:, k, :, columns(c)],
                        buffer.at[k, s],
                        send_sem.at[slot],
                        recv,
                        (g, c, k),
                    ).start()
            source = array.at[:, 1 - m, :, columns(s)]
            remote(source, buffer.at[1 - m, s], send_sem.at[slot], recv, (g, s, 1 - m)).start()
            local(array.at[:, m, :, columns(s)], buffer.at[m, s], recv).start()

    beside = s + 1 - 2 * x
    depth = weight.shape[0]
    pieces = weight_recv.shape[0]
    piece = depth // 2 // pieces

    def chunk(block, p, half=None):
        at = block * depth + (g if half is None else half) * (depth // 2) + p * piece
        return rows_all.at[pl.ds(pl.multiple_of(at, piece), piece), :]

    def whole(block):
        return rows_all.at[pl.ds(pl.multiple_of(block * depth, depth), depth), :]

    def on_line(v):
        return 2 * level(v) + x

    def post(block, p, source, where, slot):
        remote(
            source, chunk(block, p), send_sem.at[7], weight_recv.at[p, slot], (g, where, m)
        ).start()

    def over(block, p):
        view = chunk(block, p)
        remote(view, view, own_sem.at[4], plane_recv.at[p, block], (1 - g, s, m)).start()

    def landed(block, p, slot):
        take(chunk(block, p), weight_recv.at[p, slot])

    def own_piece(p):
        at = g * (depth // 2) + p * piece
        return weight.at[pl.ds(pl.multiple_of(at, piece), piece), :]

    def weight_cross(inner):
        @pl.when((above & below) if inner else jnp.logical_not(above & below))
        def _():
            for p in range(pieces):
                post(s, p, own_piece(p), on_line(3), 3)

    def weight_own():
        for p in range(pieces):
            post(s, p, own_piece(p), on_line(1), 1)
        local(weight, whole(s), whole_recv.at[0]).start()

    def weight_beside():
        for p in range(pieces):
            post(s, p, own_piece(p), beside, 4)

    def weight_near(p):
        block = on_line(1)
        landed(block, p, 1)
        post(block, p, chunk(block, p), beside, 5)
        over(block, p)

    def weight_far(p):
        block = on_line(3)
        landed(block, p, 3)
        post(block, p, chunk(block, p), on_line(1), 2)
        post(block, p, chunk(block, p), beside, 7)
        over(block, p)

    def weight_last(p):
        block = on_line(2)
        landed(block, p, 2)
        post(block, p, chunk(block, p), beside, 6)
        over(block, p)

    def weight_side(p, v):
        block = 2 * level(v) + 1 - x
        landed(block, p, 4 + v)
        over(block, p)

    def weight_end():
        take(whole(s), whole_recv.at[0])
        for p in range(pieces):
            for v in range(levels):
                for side in (x, 1 - x)[v == 0 :]:
                    block = 2 * level(v) + side
                    take(chunk(block, p, 1 - g), plane_recv.at[p, block])

    def weight_sent():
        rows = rows_all.at[pl.ds(0, 7 * (depth // 2)), :]
        take(rows, send_sem.at[7])
        take(rows, own_sem.at[4])

    def relay(buffer, which, b):
        return remote(
            buffer.at[m, b],
            buffer.at[m, b],
            send_sem.at[5 + which],
            relay_recv.at[which, b],
            (g, s, 1 - m),
        )

    def fine(buffer, which):
        def arrive(v):
            blocks = (2 * level(v) + x, 2 * level(v) + 1 - x)
            for b in blocks:
                take(buffer.at[m, b], spec_recv.at[which, b])
            return blocks

        def pass_over(b):
            relay(buffer, which, b).start()

        def passed(b):
            take(buffer.at[1 - m, b], relay_recv.at[which, b])

        fine_stage(parts, buffer, there, back_table, back, m, arrive, pass_over, passed)

    own_gate = local(gate_two, in_gate_two, recv_sem.at[4])
    own_gate = local(gate_two, in_gate_two, recv_sem.at[4])
    weight_cross(True)
    weight_own()
    weight_beside()
    hear_levels(0)

    @pl.when(above & below)
    def _():
        send_rows(signal, in_signal, 0, (3,))

    send_rows(signal, in_signal, 0, (1, 0))
    hear_levels(1)
    send_rows(signal, in_signal, 0, (2,))
    tell_levels(known_sem.at[2])

    @pl.when(jnp.logical_not(above & below))
    def _():
        pl.semaphore_wait(known_sem.at[2], 1)

    weight_cross(False)

    @pl.when(jnp.logical_not(above & below))
    def _():
        send_rows(signal, in_signal, 0, (3,))

    send_spectrum(spec_one, in_spec_one, 2, 0)

    @pl.when(above & below)
    def _():
        pl.semaphore_wait(known_sem.at[2], 2)

    build_tables(tab, there, back_table, turn, count, span)
    weight_near(0)
    weight_near(1)
    weight_side(0, 0)
    weight_side(1, 0)
    weight_far(0)
    weight_far(1)
    send_rows(gate_one, in_gate_one, 1)
    send_spectrum(spec_two, in_spec_two, 3, 1)
    weight_last(0)
    weight_last(1)
    own_gate.start()
    swap(skip_one, in_skip.at[0], 5)
    swap(skip_two, in_skip.at[1], 3)
    take(in_signal, recv_sem.at[0])
    coarse_forward(in_signal, parts, 16)
    weight_side(0, 1)
    weight_side(1, 1)
    fine(in_spec_one, 0)
    weight_side(0, 3)
    weight_side(1, 3)
    take(in_gate_one, recv_sem.at[1])
    take(in_skip.at[0], recv_sem.at[5])
    take(in_skip.at[1], recv_sem.at[3])
    mine = pl.ds(s, 1)
    coarse_back(back, in_signal, in_gate_one, in_skip[0, mine, :], second_field, 16)
    coarse_forward(second_field, parts, 16)
    weight_side(0, 2)
    weight_side(1, 2)
    fine(in_spec_two, 1)

    skip = in_skip[1, mine, :]

    width = count * cols
    tile = 2 * cols
    near, far = z // 2, 1 - z // 2

    def deliver(c, stage, own):
        return remote(
            mixed.at[c],
            arrived.at[:, columns(s)],
            own_sem.at[2] if own else send_sem.at[8],
            mix_recv.at[stage],
            (m, c, g),
        )

    def finish(low):
        wanted = range(count // 2) if low else range(count // 2, count)
        coarse_back(back, second_field, None, skip, mixed, 16, wanted)

    for stage in (1, 0):
        for low in (False, True):

            @pl.when((z < levels // 2) if low == (stage == 0) else (z >= levels // 2))
            def _():
                finish(low)

        for c in others((2, 3) if stage else (1, 0)):
            deliver(c, stage, False).start()

    @pl.when(g == m)
    def _():
        local(mixed.at[s], arrived.at[:, columns(s)], mix_recv.at[0]).start()

    @pl.when(g != m)
    def _():
        deliver(s, 0, True).start()

    def part(side):
        return pl.ds(pl.multiple_of(side * (width // 2), width // 2), width // 2)

    def gate(side, stage):
        at = part(side)
        take(arrived.at[:, at], mix_recv.at[stage])
        gated = in_gate_two[:, at].astype(jnp.float32) * arrived[:, at].astype(jnp.float32)
        features[m, :, at] = gated.astype(jnp.bfloat16)
        view = features.at[m, :, at]
        remote(view, view, send_sem.at[9], pass_recv.at[stage], (g, s, 1 - m)).start()

    def passed(side, stage):
        take(features.at[1 - m, :, part(side)], pass_recv.at[stage])

    def project(half, side, at):
        start = pl.multiple_of(half * width + side * (width // 2), width // 2)
        return jnp.dot(
            features[half, :, part(side)],
            rows_all[pl.ds(start, width // 2), at],
            preferred_element_type=jnp.float32,
        )

    def tiles(body):
        @pl.loop(0, width // tile)
        def _(i):
            body(pl.ds(pl.multiple_of(i * tile, tile), tile))

    own_gate.wait()
    gate(near, 0)
    weight_end()
    passed(near, 0)

    def first(at):
        totals[:, at] = project(m, near, at) + project(1 - m, near, at)

    tiles(first)
    gate(far, 1)

    def second(at):
        totals[:, at] += project(m, far, at)

    tiles(second)
    passed(far, 1)

    def third(at):
        out[:, at] = (totals[:, at] + project(1 - m, far, at)).astype(out.dtype)

    tiles(third)

    weight_sent()

    most = pl.ds(0, count - 1)
    for slot in (0, 1, 8):
        take(in_signal.at[most], send_sem.at[slot])
    for which in range(2):
        take(in_spec_one.at[0], send_sem.at[5 + which])
    take(arrived, send_sem.at[9])

    @pl.when(g == m)
    def _():
        for which in range(2):
            take(in_spec_one.at[:, most], send_sem.at[2 + which])
            take(in_spec_one.at[0, 0], send_sem.at[2 + which])

    @pl.when(g != m)
    def _():
        for slot in (0, 1, 2):
            take(in_signal.at[0], own_sem.at[slot])
        take(in_skip.at[0], own_sem.at[5])
        take(in_skip.at[1], own_sem.at[3])


def direct_shards(
    signal,
    gate_first,
    gate_second,
    spectrum_first,
    spectrum_second,
    skip_first,
    skip_second,
    out_weight,
):
    count = lax.axis_size("seq")
    span, width = signal.shape
    cols = width // count
    coarse = 2 * count
    strips = 2
    anywhere = pl.BlockSpec(memory_space=pltpu.HBM)
    vmem = pl.BlockSpec(memory_space=pltpu.VMEM)
    bf16, f32 = jnp.bfloat16, jnp.float32
    return pl.pallas_call(
        functools.partial(block_kernel, count),
        out_shape=jax.ShapeDtypeStruct((span, width), bf16),
        in_specs=[anywhere] * 8 + [vmem],
        out_specs=vmem,
        scratch_shapes=[
            pltpu.VMEM((count, span, cols), bf16),
            pltpu.VMEM((count, span, cols), bf16),
            pltpu.VMEM((span, width), bf16),
            pltpu.VMEM((2, count, 2, span, cols), bf16),
            pltpu.VMEM((2, count, 2, span, cols), bf16),
            pltpu.VMEM((2, count, cols), f32),
            pltpu.VMEM((coarse, 2, 2 * span, 2 * span), bf16),
            pltpu.VMEM((coarse, 2, 2 * span, 2 * span), bf16),
            pltpu.VMEM((4, span, span), f32),
            pltpu.VMEM((count + 1, 2 * span, 2 * cols), bf16),
            pltpu.VMEM((coarse, 2 * span, cols), f32),
            pltpu.VMEM((count, span, cols), bf16),
            pltpu.VMEM((count, span, cols), bf16),
            pltpu.VMEM((span, width), bf16),
            pltpu.VMEM((2, span, width), bf16),
            pltpu.VMEM((span, width), f32),
            pltpu.VMEM((2 * width, width), bf16),
            pltpu.SemaphoreType.DMA((10,)),
            pltpu.SemaphoreType.DMA((6,)),
            pltpu.SemaphoreType.DMA((6,)),
            pltpu.SemaphoreType.DMA((2, count)),
            pltpu.SemaphoreType.DMA((2, count)),
            pltpu.SemaphoreType.DMA((2, count)),
            pltpu.SemaphoreType.DMA((2, count)),
            pltpu.SemaphoreType.DMA((1,)),
            pltpu.SemaphoreType.REGULAR((count // 2 - 1,)),
            pltpu.SemaphoreType.DMA((strips,)),
            pltpu.SemaphoreType.DMA((strips,)),
        ],
        compiler_params=pltpu.CompilerParams(
            collective_id=0, has_side_effects=True, vmem_limit_bytes=62 * 1024 * 1024
        ),
        cost_estimate=pl.CostEstimate(
            flops=16 * coarse * span * span * cols, bytes_accessed=1 << 26, transcendentals=0
        ),
    )(
        signal,
        gate_first,
        gate_second,
        spectrum_first,
        spectrum_second,
        skip_first.reshape(count, cols),
        skip_second.reshape(count, cols),
        out_weight,
        jnp.asarray(turn_tables(span, coarse)),
    )


def shards(*arrays):
    count = lax.axis_size("seq")
    span, width = arrays[0].shape
    pairs = lax.axis_size("grp") == 2 and lax.axis_size("mdl") == 2
    whole_tiles = width == count * LANES and span == LANES and count == 8
    if pairs and whole_tiles and arrays[3].shape[1] == 2:
        return direct_shards(*arrays)
    return plain_shards(*arrays)


def solution(mesh):
    placed = (
        P(("grp", "seq"), "mdl"),
        P(("grp", "seq"), "mdl"),
        P(("grp", "seq"), "mdl"),
        P(None, "seq", None, "mdl"),
        P(None, "seq", None, "mdl"),
        P("mdl"),
        P("mdl"),
        P("seq", "mdl"),
    )
    return jax.shard_map(
        shards, mesh=mesh, in_specs=placed, out_specs=P(("grp", "seq"), "mdl"), check_vma=False
    )
```
